128 devices in a mesh: lat: 8 (over x, core), lon: 16 (over y, z).
Axes of the slice: x: 4, y: 4, z: 4, core: 2. Of those that a mesh axis runs over, the one named last changes fastest.
Arguments:
- prior: float32 [1024, 32768], P('lat', 'lon'), may hold values from 0.005 to 120
- zone_ids: int32 [1024, 32768], P('lat', 'lon'), may hold values from 0 to 4095, as said below
- rate: float32 [4096], replicated, may hold values from 0.3 to 3
Outputs:
- density: float32 [1024, 32768], P('lat', 'lon')
The draws below stay inside these ranges and needn't reach their ends.
Inputs may be any that keep to these rules, and one draw needn't show every extreme that they name: `zone_ids`: provinces are unions of aligned blocks of 8 rows by 64 columns, except that in the last 16 columns of a block some cells take the province of the block to the east (longitude wrapping); every province owns at least one whole block.
All inputs are finite; a program needn't handle non-finite values.
Results may differ from the reference program's by a relative error of at most 0.0002.
Values sent between devices are 32-bit elements; how exact they have to be, the bound alone decides.
A program may use at most 64 MiB of HBM per device.

```python
import math
import jax
import jax.numpy as jnp

ZONES = 4096
ROUNDS = 2
SWEEPS = 3
NLAT = 1024
NLON = 32768


def draw_prior(key, part):
    block_rows = NLAT // 8
    block_cols = NLON // 64
    keys = jax.random.split(key, 3)
    pick = jax.random.uniform(keys[0], (block_rows, block_cols), jnp.float32)
    level = jnp.where(pick < 0.5, 0.25, 4.0)
    row_factor = jnp.exp(jax.random.uniform(keys[1], (NLAT, 1), jnp.float32, math.log(0.25), math.log(4.0)))
    cell = jnp.exp(jax.random.uniform(keys[2], (NLAT, NLON), jnp.float32, math.log(0.2), math.log(5.0)))
    blocks = jnp.repeat(jnp.repeat(level, 8, axis=0), 64, axis=1)
    return (blocks * row_factor * cell).astype(jnp.float32)


def draw_zone_ids(key, part):
    block_rows = NLAT // 8
    block_cols = NLON // 64
    blocks = block_rows * block_cols
    keys = jax.random.split(key, 5)
    ranking = jax.random.permutation(keys[0], blocks).astype(jnp.int32)
    first = jax.random.randint(keys[1], (blocks,), 0, ZONES)
    second = jax.random.randint(keys[2], (blocks,), 0, ZONES)
    third = jax.random.randint(keys[3], (blocks,), 0, ZONES)
    common = jnp.minimum(jnp.minimum(first, second), third)
    zone_block = jnp.where(ranking < ZONES, ranking, common).reshape(block_rows, block_cols)
    east_block = jnp.roll(zone_block, -1, axis=1)
    cells = jnp.repeat(jnp.repeat(zone_block, 8, axis=0), 64, axis=1)
    east_cells = jnp.repeat(jnp.repeat(east_block, 8, axis=0), 64, axis=1)
    column = jnp.arange(NLON) % 64
    flips = jax.random.randint(keys[4], (NLAT, NLON), 0, 2)
    taken = (column >= 48)[None, :] & (flips == 1)
    return jnp.where(taken, east_cells, cells).astype(jnp.int32)


def setup_inputs(seed: int = 0) -> dict:
    key_of = jax.random.split(jax.random.key(seed), 4)
    prior = draw_prior(jax.random.fold_in(key_of[3], 71), 0)
    zone_ids = draw_zone_ids(jax.random.fold_in(key_of[3], 71), 0)
    rate = jnp.clip(jnp.exp(jax.random.uniform(key_of[2], (ZONES,), jnp.float32, math.log(0.3), math.log(3.0))), 0.3, 3.0)
    return {"prior": prior, "zone_ids": zone_ids, "rate": rate}


def sweep(s):
    north = jnp.concatenate([s[:1], s[:-1]], axis=0)
    south = jnp.concatenate([s[1:], s[-1:]], axis=0)
    east = jnp.roll(s, -1, axis=1)
    west = jnp.roll(s, 1, axis=1)
    return 0.2 * (s + north + south + east + west)


def reference(prior, zone_ids, rate):
    flat_ids = zone_ids.reshape(-1)
    counts = jax.ops.segment_sum(jnp.ones(flat_ids.shape, jnp.float32), flat_ids, num_segments=ZONES)
    target = rate * counts
    state = prior
    for round_index in range(ROUNDS):
        for sweep_index in range(SWEEPS):
            state = sweep(state)
        sums = jax.ops.segment_sum(state.reshape(-1), flat_ids, num_segments=ZONES)
        factor = target / sums
        state = state * factor[zone_ids]
    return state
```

```python
import jax
import jax.numpy as jnp
from jax import lax
from jax.experimental import pallas as pl
from jax.experimental.pallas import tpu as pltpu
from jax.sharding import PartitionSpec as P

ZONES = 4096
SWEEPS = 3
ROWS, COLS = 128, 2048
PLANES = 16
TILES = COLS // 128
WIDE = COLS + 128
DEPTH = 6
IDS = 3
MESH = pl.DeviceIdType.MESH
F32, I32, BF16 = jnp.float32, jnp.int32, jnp.bfloat16


def split2(x):
    high = x.astype(BF16)
    low = (x - high.astype(F32)).astype(BF16)
    return jnp.concatenate([high, low], axis=0)


def place(row, col):
    return {"lat": lax.rem(row + 8, 8), "lon": lax.rem(col + 16, 16)}


def device(x, core, y, z):
    return (lax.rem(x, 4) * 2 + core, lax.rem(y, 4) * 4 + lax.rem(z, 4))


FAR_A = [2, 3, 1, 0]
FAR_B = sorted(
    [(a, b) for a in range(4) for b in range(4) if (a, b) != (0, 0)],
    key=lambda t: -(min(t[0], 4 - t[0]) + min(t[1], 4 - t[1])),
)


def kernel(
    prior, zones, rate, out,
    pin, zin, state, halo, ids, hids, own, wide_out,
    prow, pcol, pcorner, zrow, zcol, zcorner, ppack, zpack,
    spread, onehot_hi, onehot_lo,
    part, part_in, half, half_in, factors,
    load_sem, store_sem, halo_send, halo_recv, zhalo_send, zhalo_recv,
    a_send, a_recv, b_send, b_recv, c_send, c_recv,
):
    lat, lon = lax.axis_index("lat"), lax.axis_index("lon")
    x, core = lax.div(lat, 2), lax.rem(lat, 2)
    y, z = lax.div(lon, 4), lax.rem(lon, 4)
    sent = []

    around = [(-1, 0), (1, 0), (0, -1), (0, 1), (-1, -1), (-1, 1), (1, -1), (1, 1)]
    a_peers = []
    for d in FAR_A:
        for flip in (1, 0):
            if (d, flip) != (0, 0):
                a_peers.append((d * 2 + flip, flip, device(x + d, jnp.where(flip == 1, 1 - core, core), y, z)))
    b_peers = [(i, device(x, core, y + a, z + b)) for i, (a, b) in enumerate(FAR_B)]
    partner = device(x, 1 - core, y, z)

    barrier = pltpu.get_barrier_semaphore()
    greeted = 0
    for dr, dc in around:
        pl.semaphore_signal(barrier, inc=1, device_id=place(lat + dr, lon + dc), device_id_type=MESH)
        greeted += 1
    for _, _, peer in a_peers:
        pl.semaphore_signal(barrier, inc=1, device_id=peer, device_id_type=MESH)
        greeted += 1
    for _, peer in b_peers:
        pl.semaphore_signal(barrier, inc=1, device_id=peer, device_id_type=MESH)
        greeted += 1

    def tile(t):
        return slice(128 * t, 128 * t + 128)

    loads = [[None] * TILES, [None] * TILES]
    for n, t in [(0, 0), (0, TILES - 1), (1, 0), (1, TILES - 1)] + [(n, t) for t in range(1, TILES - 1) for n in (1, 0)]:
        copy = pltpu.make_async_copy((prior, zones)[n].at[:, tile(t)], (pin, zin)[n].at[t], load_sem.at[n, t])
        copy.start()
        loads[n][t] = copy

    sub = lax.broadcasted_iota(I32, (8, 128), 0)
    lane = lax.broadcasted_iota(I32, (8, 128), 1)
    upper = (lane >= 64).astype(I32)

    def pick(value, index):
        return jnp.take_along_axis(value, index, axis=1, mode="promise_in_bounds")

    def plane_of(ref, p, t):
        return ref.at[t][pl.ds(p, 8, stride=PLANES), :]

    def pack(ref, packed):
        west, east = jnp.zeros((8, 128), packed.dtype), jnp.zeros((8, 128), packed.dtype)
        for p in range(PLANES):
            mine = (lane >= 8 * p) & (lane < 8 * p + 8)
            west = jnp.where(mine, pltpu.roll(plane_of(ref, p, 0), 8 * p, 1), west)
            east = jnp.where(mine, pltpu.roll(plane_of(ref, p, TILES - 1), (8 * p + 8) % 128, 1), east)
        packed[0] = west
        packed[1] = east

    def send_halo(source, packed, row_in, col_in, corner_in, send, recv):
        first8, last8 = pl.ds(0, 8), pl.ds(ROWS - 8, 8)
        first128, last128 = pl.ds(0, 128), pl.ds(COLS - 128, 128)
        plan = [
            (source.at[first8, first128], corner_in.at[2], (-1, -1)),
            (source.at[first8, last128], corner_in.at[3], (-1, 1)),
            (source.at[last8, first128], corner_in.at[0], (1, -1)),
            (source.at[last8, last128], corner_in.at[1], (1, 1)),
            (packed.at[0], col_in.at[0], (0, -1)),
            (packed.at[1], col_in.at[1], (0, 1)),
            (source.at[first8, :], row_in.at[1], (-1, 0)),
            (source.at[last8, :], row_in.at[0], (1, 0)),
        ]
        copies = []
        for n, (src, dst, (dr, dc)) in enumerate(plan):
            copy = pltpu.make_async_remote_copy(
                src_ref=src, dst_ref=dst, send_sem=send.at[n], recv_sem=recv.at[n],
                device_id=place(lat + dr, lon + dc), device_id_type=MESH,
            )
            copy.start()
            copies.append(copy)
        sent.extend(copies)
        return copies

    loads[0][0].wait()
    loads[0][TILES - 1].wait()
    pack(pin, ppack)
    pl.semaphore_wait(barrier, greeted)
    halo_copies = send_halo(prior, ppack, prow, pcol, pcorner, halo_send, halo_recv)
    loads[1][0].wait()
    loads[1][TILES - 1].wait()
    pack(zin, zpack)
    zhalo_copies = send_halo(zones, zpack, zrow, zcol, zcorner, zhalo_send, zhalo_recv)
    for t in range(1, TILES - 1):
        loads[1][t].wait()
        loads[0][t].wait()

    for t in range(TILES):
        for p in range(PLANES):
            ids[p, :, tile(t)] = plane_of(zin, p, t)
            state[0, p, :, tile(t)] = plane_of(pin, p, t)

    def own_of(first):
        packed = jnp.full((8, 128), -1, I32)
        cells = []
        for t in range(TILES):
            value = first(t)
            packed = jnp.where(lax.div(lax.rem(lane, 32), 2) == t, pick(value, 64 * lax.rem(lane, 2)), packed)
            cells.append(pick(value, 64 * upper))
        return packed, cells

    packed_own = []
    east_ext = []
    for h in range(2):
        packed, cells = own_of(lambda t: ids[8 * h, :, tile(t)])
        packed_own.append(packed)
        for t in range(TILES):
            own[h, :, tile(t)] = cells[t]
        other = jnp.full((8, 128), -1, I32)
        for p in range(8 * h, 8 * h + 8):
            value = ids[p, :, tile(TILES - 1)]
            other = jnp.maximum(other, jnp.where(value == cells[-1], -1, value))
        other = jnp.where(lane >= 64, other, -1)
        east_ext.append(jnp.max(other, axis=1, keepdims=True))
    entries = jnp.where(lane < 32, packed_own[0], packed_own[1])
    entries = jnp.where(lane < 64, entries, jnp.where(lane == 64, east_ext[0], jnp.where(lane == 65, east_ext[1], -1)))

    hi_iota = lax.broadcasted_iota(I32, (32, 128), 0)
    lo_iota = lax.broadcasted_iota(I32, (128, 128), 0)

    def encode(entry_ids, row, group):
        line = entry_ids[row : row + 1, :]
        hi = jnp.right_shift(line, 7)
        lo = jnp.bitwise_and(line, 127)
        onehot_hi[group] = jnp.where(hi_iota == hi, 1.0, 0.0)
        onehot_lo[:, 128 * group : 128 * group + 128] = jnp.where(lo_iota == lo, 1.0, 0.0).astype(BF16)

    for s in range(8):
        encode(entries, s, s)
    column_block = lax.div(lax.broadcasted_iota(I32, (COLS, 128), 0), 64)
    lane_block = lax.rem(lax.broadcasted_iota(I32, (COLS, 128), 1), 32)
    spread[...] = jnp.where(column_block == lane_block, 1.0, 0.0).astype(BF16)

    def zone_totals(value_of):
        for h in range(2):
            for q in range(4):
                columns = slice(512 * q, 512 * q + 512)
                mine = own[h, :, columns]
                own_sum, east_sum = jnp.zeros((8, 512), F32), jnp.zeros((8, 512), F32)
                for p in range(8 * h, 8 * h + 8):
                    matched = ids[p, :, columns] == mine
                    value = value_of(p, columns)
                    own_sum += jnp.where(matched, value, 0.0)
                    east_sum += jnp.where(matched, 0.0, value)
                wide_out[8 * h : 8 * h + 8, columns] = own_sum
                wide_out[16 + 8 * h : 24 + 8 * h, columns] = east_sum
        lanes = jnp.dot(split2(wide_out[0:32, :]), spread[...], preferred_element_type=F32)
        lanes = lanes[0:32] + lanes[32:64]
        own0, own1, east0, east1 = lanes[0:8], lanes[8:16], lanes[16:24], lanes[24:32]
        next0, next1 = pltpu.roll(east0, 1, 1), pltpu.roll(east1, 1, 1)
        sums = jnp.where(lane < 32, own0 + jnp.where(lane >= 1, next0, 0.0), own1 + jnp.where(lane > 32, next1, 0.0))
        ext = jnp.where(lane == 64, next0, jnp.where(lane == 65, pltpu.roll(east1, 2, 1), 0.0))
        sums = jnp.where(lane < 64, sums, ext)
        weighted = [onehot_hi[s] * sums[s : s + 1, :] for s in range(8)]
        weighted = split2(jnp.concatenate(weighted, axis=1))
        table = lax.dot_general(
            weighted, onehot_lo[:, 0:1024], (((1,), (1,)), ((), ())), preferred_element_type=F32
        )
        return table[0:32] + table[32:64]

    def start_a(n, table):
        part[n] = table.reshape(2, 16, 128)
        copies = []
        for slot, flip, peer in a_peers:
            copy = pltpu.make_async_remote_copy(
                src_ref=part.at[n, 1 - core if flip else core], dst_ref=part_in.at[n, slot],
                send_sem=a_send.at[n, slot], recv_sem=a_recv.at[n, slot],
                device_id=peer, device_id_type=MESH,
            )
            copy.start()
            copies.append((slot, copy))
        sent.extend(copy for _, copy in copies)
        return copies

    def start_b(n, copies):
        total = part[n, core]
        for slot, copy in reversed(copies):
            copy.wait_recv()
            total += part_in[n, slot]
        half[n] = total
        copies = []
        for i, peer in b_peers:
            copy = pltpu.make_async_remote_copy(
                src_ref=half.at[n], dst_ref=half_in.at[n, i],
                send_sem=b_send.at[n, i], recv_sem=b_recv.at[n, i],
                device_id=peer, device_id_type=MESH,
            )
            copy.start()
            copies.append((i, copy))
        sent.extend(copy for _, copy in copies)
        return copies, total

    def finish_b(n, started):
        copies, total = started
        for i, copy in reversed(copies):
            copy.wait_recv()
            total += half_in[n, i]
        return total

    def share(n, factor):
        factors[n, core] = factor
        copy = pltpu.make_async_remote_copy(
            src_ref=factors.at[n, core], dst_ref=factors.at[n, core],
            send_sem=c_send.at[n], recv_sem=c_recv.at[n],
            device_id=partner, device_id_type=MESH,
        )
        copy.start()
        sent.append(copy)
        copy.wait_recv()
        return factors[n].reshape(32, 128)

    counting = start_a(0, zone_totals(lambda p, columns: jnp.ones((8, 512), F32)))

    def fill_halo(copies, row_in, col_in, corner_in, planes, halo_planes, depth):
        for copy in copies:
            copy.wait_recv()
        for p in range(PLANES):
            east = pltpu.roll(col_in[0], (128 - 8 * p) % 128, 1)
            west = pltpu.roll(col_in[1], (120 - 8 * p) % 128, 1)
            planes[p, :, COLS:WIDE] = jnp.where(lane < 64, east, west)
        sub_wide = lax.broadcasted_iota(I32, (8, WIDE), 0)
        for k in range(1, depth + 1):
            lines = []
            for side, row in ((0, 8 - k), (1, k - 1)):
                edge = jnp.where(
                    lane[0:1] < 64, corner_in[2 * side, row : row + 1, :], corner_in[2 * side + 1, row : row + 1, :]
                )
                lines.append(jnp.concatenate([row_in[side, row : row + 1, :], edge], axis=1))
            top = jnp.where(lat == 0, planes[k - 1], jnp.broadcast_to(lines[0], (8, WIDE)))
            bottom = jnp.where(lat == 7, planes[PLANES - k], jnp.broadcast_to(lines[1], (8, WIDE)))
            halo_planes[k - 1] = jnp.where(sub_wide < 4, top, bottom)

    fill_halo(halo_copies, prow, pcol, pcorner, state.at[0], halo.at[0], DEPTH)

    def smooth(src, dst, depth):
        sub_wide = lax.broadcasted_iota(I32, (8, WIDE), 0)

        def stencil(centre, one, other):
            beside = pltpu.roll(centre, 1, 1) + pltpu.roll(centre, WIDE - 1, 1)
            return 0.2 * (centre + (one + other) + beside)

        for p in range(PLANES):
            centre = state[src, p]
            if p == 0:
                north = jnp.where(sub_wide == 0, halo[src, 0], pltpu.roll(state[src, PLANES - 1], 1, 0))
            else:
                north = state[src, p - 1]
            if p == PLANES - 1:
                south = jnp.where(sub_wide == 7, halo[src, 0], pltpu.roll(state[src, 0], 7, 0))
            else:
                south = state[src, p + 1]
            state[dst, p] = stencil(centre, north, south)
        for k in range(1, depth):
            if k == 1:
                inner = jnp.where(sub_wide < 4, state[src, 0], state[src, PLANES - 1])
            else:
                inner = halo[src, k - 2]
            halo[dst, k - 1] = stencil(halo[src, k - 1], inner, halo[src, k])

    for n in range(SWEEPS):
        smooth(n % 2, (n + 1) % 2, DEPTH - n)

    counting = start_b(0, counting)
    summing = start_a(1, zone_totals(lambda p, columns: state[1, p, :, columns]))

    fill_halo(zhalo_copies, zrow, zcol, zcorner, ids, hids, IDS)
    zero = jnp.zeros((8, 128), I32)

    def far_ids(values, own0):
        other = jnp.full((8, 128), -1, I32)
        for value in values:
            other = jnp.maximum(other, jnp.where(value == own0, -1, value))
        return jnp.max(jnp.where(lane >= 125, other, -1), axis=1, keepdims=True)

    for h in range(2):
        own0 = pick(own[h, :, tile(0)], zero)
        own[h, :, tile(TILES)] = own0
        west = far_ids([ids[p, :, tile(TILES)] for p in range(8 * h, 8 * h + 8)], own0)
        east = pick(ids[8 * h, :, tile(TILES)], zero)
        entries = jnp.where(lane == 66 + h, west, jnp.where(lane == 68 + h, east, entries))
    packed, cells = own_of(lambda t: hids[0, :, tile(t)])
    for t in range(TILES):
        own[2, :, tile(t)] = cells[t]
    own0 = pick(hids[0, :, tile(0)], zero)
    own[2, :, tile(TILES)] = own0
    west = far_ids([hids[k, :, tile(TILES)] for k in range(IDS)], own0)
    east = pick(hids[0, :, tile(TILES)], zero)
    hentries = jnp.where(lane < 32, packed, -1)
    hentries = jnp.where(lane == 66, west, jnp.where((lane == 64) | (lane == 68), east, hentries))

    summing = start_b(1, summing)
    for s in range(8):
        encode(entries, s, s)
    encode(hentries, 0, 8)
    encode(hentries, 7, 9)

    count = finish_b(0, counting)
    target = rate[core] * count

    def lookup(table, groups):
        rows = jnp.dot(split2(table), onehot_lo[:, 0 : 128 * groups], preferred_element_type=F32)
        rows = rows[0:32] + rows[32:64]
        lines = []
        for g in range(groups):
            lines.append(jnp.sum(rows[:, 128 * g : 128 * g + 128] * onehot_hi[g], axis=0, keepdims=True))
        return lines

    def cell_factors(values, h, t):
        if t < TILES:
            mine = 32 * h + 2 * t + upper
            east = mine + 1 if t < TILES - 1 else jnp.where(upper == 1, 64 + h, mine + 1)
        else:
            mine = jnp.where(upper == 1, 32 * h, 68 + h)
            east = jnp.where(upper == 1, 66 + h, 68 + h)
        return pick(values, mine), pick(values, east)

    lines = lookup(share(0, target / finish_b(1, summing)), 10)
    values = jnp.concatenate(lines[0:8], axis=0)
    hvalues = jnp.where(sub < 4, lines[8], lines[9])
    for t in range(TILES + 1):
        for h in range(2):
            mine, east = cell_factors(values, h, t)
            own_ids = own[h, :, tile(t)]
            for p in range(8 * h, 8 * h + 8):
                scale = jnp.where(ids[p, :, tile(t)] == own_ids, mine, east)
                state[1, p, :, tile(t)] = state[1, p, :, tile(t)] * scale
        mine, east = cell_factors(hvalues, 0, t)
        own_ids = own[2, :, tile(t)]
        for k in range(IDS):
            scale = jnp.where(hids[k, :, tile(t)] == own_ids, mine, east)
            halo[1, k, :, tile(t)] = halo[1, k, :, tile(t)] * scale

    for n in range(SWEEPS):
        smooth((n + 1) % 2, n % 2, SWEEPS - n)

    summing = start_b(2, start_a(2, zone_totals(lambda p, columns: state[0, p, :, columns])))
    lines = lookup(share(1, target / finish_b(2, summing)), 8)
    values = jnp.concatenate(lines, axis=0)
    stores = []
    for t in range(TILES):
        for h in range(2):
            mine, east = cell_factors(values, h, t)
            own_ids = own[h, :, tile(t)]
            for p in range(8 * h, 8 * h + 8):
                scale = jnp.where(ids[p, :, tile(t)] == own_ids, mine, east)
                pin.at[t][pl.ds(p, 8, stride=PLANES), :] = state[0, p, :, tile(t)] * scale
        copy = pltpu.make_async_copy(pin.at[t], out.at[:, tile(t)], store_sem.at[t])
        copy.start()
        stores.append(copy)
    for copy in sent:
        copy.wait_send()
    for copy in stores:
        copy.wait()


def body(prior, zone_ids, rate):
    dma = pltpu.SemaphoreType.DMA
    vmem = pltpu.VMEM
    anywhere = pl.BlockSpec(memory_space=pl.ANY)
    return pl.pallas_call(
        kernel,
        out_shape=jax.ShapeDtypeStruct((ROWS, COLS), F32),
        in_specs=[anywhere, anywhere, pl.BlockSpec(memory_space=pltpu.VMEM)],
        out_specs=anywhere,
        scratch_shapes=[
            vmem((TILES, ROWS, 128), F32),
            vmem((TILES, ROWS, 128), I32),
            vmem((2, PLANES, 8, WIDE), F32),
            vmem((2, DEPTH, 8, WIDE), F32),
            vmem((PLANES, 8, WIDE), I32),
            vmem((IDS, 8, WIDE), I32),
            vmem((3, 8, WIDE), I32),
            vmem((32, COLS), F32),
            vmem((2, 8, COLS), F32),
            vmem((2, 8, 128), F32),
            vmem((4, 8, 128), F32),
            vmem((2, 8, COLS), I32),
            vmem((2, 8, 128), I32),
            vmem((4, 8, 128), I32),
            vmem((2, 8, 128), F32),
            vmem((2, 8, 128), I32),
            vmem((COLS, 128), BF16),
            vmem((10, 32, 128), F32),
            vmem((128, 1280), BF16),
            vmem((3, 2, 16, 128), F32),
            vmem((3, 8, 16, 128), F32),
            vmem((3, 16, 128), F32),
            vmem((3, 15, 16, 128), F32),
            vmem((2, 2, 16, 128), F32),
            dma((2, TILES)),
            dma((TILES,)),
            dma((8,)),
            dma((8,)),
            dma((8,)),
            dma((8,)),
            dma((3, 8)),
            dma((3, 8)),
            dma((3, 15)),
            dma((3, 15)),
            dma((2,)),
            dma((2,)),
        ],
        compiler_params=pltpu.CompilerParams(
            collective_id=0, has_side_effects=True, vmem_limit_bytes=48 * 1024 * 1024
        ),
    )(prior, zone_ids, rate.reshape(2, 16, 128))


def solution(mesh):
    placed = (P("lat", "lon"), P("lat", "lon"), P())
    return jax.shard_map(
        body, mesh=mesh, in_specs=placed, out_specs=P("lat", "lon"), check_vma=False
    )
```

```python
import jax
import jax.numpy as jnp
from jax import lax
from jax.experimental import pallas as pl
from jax.experimental.pallas import tpu as pltpu
from jax.sharding import PartitionSpec as P

ROWS, COLS = 128, 2048
STEP = 16
TILES = COLS // 128
SWEEPS = 3
DEPTH = 6
IDS = 3
SIDE = STEP + DEPTH
GROUPS = 10
MESH = pl.DeviceIdType.MESH
F32, I32, BF16 = jnp.float32, jnp.int32, jnp.bfloat16


def split2(x):
    high = x.astype(BF16)
    low = (x - high.astype(F32)).astype(BF16)
    return jnp.concatenate([high, low], axis=0)


def place(row, col):
    return {"lat": lax.rem(row + 8, 8), "lon": lax.rem(col + 16, 16)}


def device(x, core, y, z):
    return (lax.rem(x, 4) * 2 + core, lax.rem(y, 4) * 4 + lax.rem(z, 4))


FAR_A = [2, 3, 1, 0]
FAR_B = sorted(
    [(a, b) for a in range(4) for b in range(4) if (a, b) != (0, 0)],
    key=lambda t: -(min(t[0], 4 - t[0]) + min(t[1], 4 - t[1])),
)


def drain(ref, sem):
    pltpu.make_async_copy(ref, ref, sem).wait()


def kernel(
    prior, zones, rate, out,
    pin, zin, turn, iturn, level, ids,
    prow, pcol, pcorner, zrow, zcol, zcorner, ppack, zpack,
    onehot_hi, onehot_lo,
    part, part_in, half, half_in, factors,
    load_sem, store_sem, rate_sem, halo_send, halo_recv, zhalo_send, zhalo_recv,
    a_send, a_recv, b_send, b_recv, c_send, c_recv, rate_in,
):
    lat, lon = lax.axis_index("lat"), lax.axis_index("lon")
    x, core = lax.div(lat, 2), lax.rem(lat, 2)
    y, z = lax.div(lon, 4), lax.rem(lon, 4)

    around = [(-1, 0), (1, 0), (0, -1), (0, 1), (-1, -1), (-1, 1), (1, -1), (1, 1)]
    a_peers = []
    for d in FAR_A:
        for flip in (1, 0):
            if (d, flip) != (0, 0):
                a_peers.append((d * 2 + flip, flip, device(x + d, jnp.where(flip == 1, 1 - core, core), y, z)))
    b_peers = [(i, device(x, core, y + a, z + b)) for i, (a, b) in enumerate(FAR_B)]
    partner = device(x, 1 - core, y, z)

    barrier = pltpu.get_barrier_semaphore()
    greeted = 0
    for dr, dc in around:
        pl.semaphore_signal(barrier, inc=1, device_id=place(lat + dr, lon + dc), device_id_type=MESH)
        greeted += 1

    def tile(t):
        return slice(128 * t, 128 * t + 128)

    for n, t in [(0, 0), (0, TILES - 1), (1, 0), (1, TILES - 1)] + [(n, t) for n in (0, 1) for t in range(1, TILES - 1)]:
        sem = load_sem.at[n, 0 if t == 0 else 1 if t == TILES - 1 else 2]
        pltpu.make_async_copy((prior, zones)[n].at[:, tile(t)], (pin, zin)[n].at[t], sem).start()
    rate_copy = pltpu.make_async_copy(rate, rate_in, rate_sem)
    rate_copy.start()

    for _, _, peer in a_peers:
        pl.semaphore_signal(barrier, inc=1, device_id=peer, device_id_type=MESH)
        greeted += 1
    for _, peer in b_peers:
        pl.semaphore_signal(barrier, inc=1, device_id=peer, device_id_type=MESH)
        greeted += 1

    lane = lax.broadcasted_iota(I32, (8, 128), 1)
    q = lax.broadcasted_iota(I32, (8, 128), 0)
    s = lax.rem(lane, 8)
    mirror_top = s + 8 * lat < 4
    mirror_bottom = s + 8 * lat >= 60

    def pick(value, index):
        return jnp.take_along_axis(value, index, axis=1, mode="promise_in_bounds")

    def spread(row, shape=(8, 128)):
        return jnp.broadcast_to(row, shape)

    def pack(ref, packed):
        index = 16 * s + lax.div(lane, 8)
        packed[0] = pick(ref[0].T[0:8], index)
        packed[1] = pick(ref[TILES - 1].T[120:128], index)

    first8, last8 = pl.ds(0, 8), pl.ds(ROWS - 8, 8)
    first128, last128 = pl.ds(0, 128), pl.ds(COLS - 128, 128)

    def send(src, dst, send_sem, recv_sem, dr, dc):
        pltpu.make_async_remote_copy(
            src_ref=src, dst_ref=dst, send_sem=send_sem, recv_sem=recv_sem,
            device_id=place(lat + dr, lon + dc), device_id_type=MESH,
        ).start()

    def send_rows(source, row_in, corner_in, out_sem, in_sem):
        send(source.at[first8, first128], corner_in.at[2], out_sem.at[2], in_sem.at[2], -1, -1)
        send(source.at[first8, last128], corner_in.at[3], out_sem.at[2], in_sem.at[2], -1, 1)
        send(source.at[last8, first128], corner_in.at[0], out_sem.at[2], in_sem.at[2], 1, -1)
        send(source.at[last8, last128], corner_in.at[1], out_sem.at[2], in_sem.at[2], 1, 1)
        send(source.at[first8, :], row_in.at[1], out_sem.at[0], in_sem.at[0], -1, 0)
        send(source.at[last8, :], row_in.at[0], out_sem.at[0], in_sem.at[0], 1, 0)

    def send_cols(packed, col_in, out_sem, in_sem):
        send(packed.at[0], col_in.at[0], out_sem.at[1], in_sem.at[1], 0, -1)
        send(packed.at[1], col_in.at[1], out_sem.at[1], in_sem.at[1], 0, 1)

    drain(pin.at[0], load_sem.at[0, 0])
    drain(pin.at[TILES - 1], load_sem.at[0, 1])
    pack(pin, ppack)
    pl.semaphore_wait(barrier, greeted)
    send_cols(ppack, pcol, halo_send, halo_recv)
    send_rows(prior, prow, pcorner, halo_send, halo_recv)
    drain(zin.at[0], load_sem.at[1, 0])
    drain(zin.at[TILES - 1], load_sem.at[1, 1])
    pack(zin, zpack)
    send_cols(zpack, zcol, zhalo_send, zhalo_recv)
    send_rows(zones, zrow, zcorner, zhalo_send, zhalo_recv)

    inner = pl.ds(1, TILES - 2)

    def turned(matrix, slot):
        buffer = turn if matrix.dtype == F32 else iturn
        buffer[slot] = matrix.T
        return [buffer.at[slot][pl.ds(t, 8, stride=STEP), :] for t in range(STEP)]

    def load_planes(ref, write):
        for r in range(STEP):
            rows = [ref.at[t][pl.ds(r, 8, stride=STEP), :] for t in range(TILES)]
            for t, value in enumerate(turned(jnp.concatenate(rows, axis=0), r % 4)):
                write(r, t, value)

    def write_prior(r, t, value):
        level[0, r, t] = value

    def write_ids(r, t, value):
        ids[r, t] = value

    drain(pin.at[inner], load_sem.at[0, 2])
    load_planes(pin, write_prior)
    drain(zin.at[inner], load_sem.at[1, 2])
    load_planes(zin, write_ids)

    hi_iota = lax.broadcasted_iota(I32, (32, 128), 0)
    lo_iota = lax.broadcasted_iota(I32, (128, 128), 0)

    def encode(line, group):
        hi = jnp.right_shift(line, 7)
        lo = jnp.bitwise_and(line, 127)
        onehot_hi[group] = jnp.where(hi_iota == hi, 1.0, 0.0)
        onehot_lo[:, 128 * group : 128 * group + 128] = jnp.where(lo_iota == lo, 1.0, 0.0).astype(BF16)

    def own_ids(row):
        value = ids[row, 0]
        return [value[0:1], value[4:5]], jnp.where(q < 4, spread(value[0:1]), spread(value[4:5]))

    own = []
    for h in range(2):
        lines, cells = own_ids(8 * h)
        own.append(cells)
        for g in range(2):
            encode(lines[g], 2 * h + g)

    def fold(value):
        value = value + pltpu.roll(value, 7, 0)
        value = value + pltpu.roll(value, 6, 0)
        return value[0:1], value[4:5]

    def scatter(pairs):
        lines, ext = [], []
        for own_sum, east_sum in pairs:
            own0, own1 = fold(own_sum)
            east0, east1 = fold(east_sum)
            east1 = spread(east1)
            beyond = pltpu.roll(east1, 8, 1)[0:1]
            lines.append(own0 + jnp.where(lane[0:1] >= 8, beyond, 0.0))
            lines.append(own1 + east0)
            ext.append((east1[0:1], beyond))
        lines.append(jnp.where(lane[0:1] >= 120, ext[0][0], jnp.where(lane[0:1] < 8, ext[1][1], 0.0)))
        weighted = split2(jnp.concatenate([onehot_hi[g] * lines[g] for g in range(5)], axis=1))
        table = lax.dot_general(
            weighted, onehot_lo[:, 0:640], (((1,), (1,)), ((), ())), preferred_element_type=F32
        )
        return table[0:32] + table[32:64]

    def block_sums(n, h):
        own_sum, east_sum = jnp.zeros((STEP, 8, 128), F32), jnp.zeros((STEP, 8, 128), F32)
        for r in range(8 * h, 8 * h + 8):
            matched = ids[r, 0:STEP] == own[h]
            value = level[n, r, 0:STEP]
            own_sum += jnp.where(matched, value, 0.0)
            east_sum += jnp.where(matched, 0.0, value)
        return jnp.sum(own_sum, axis=0), jnp.sum(east_sum, axis=0)

    counts, others = [], []
    for h in range(2):
        own_sum = jnp.zeros((STEP, 8, 128), F32)
        other = jnp.full((STEP, 8, 128), -1, I32)
        for r in range(8 * h, 8 * h + 8):
            value = ids[r, 0:STEP]
            matched = value == own[h]
            own_sum += jnp.where(matched, 1.0, 0.0)
            other = jnp.maximum(other, jnp.where(matched, -1, value))
        own_sum = jnp.sum(own_sum, axis=0)
        counts.append((own_sum, float(8 * STEP) - own_sum))
        others.append(spread(jnp.max(other, axis=0)[7:8]))
    encode(jnp.where(lane >= 120, others[0], jnp.where(lane < 8, pltpu.roll(others[1], 8, 1), -1))[0:1], 4)

    def start_a(n, table):
        part[n] = table.reshape(2, 16, 128)
        for slot, flip, peer in a_peers:
            pltpu.make_async_remote_copy(
                src_ref=part.at[n, 1 - core if flip else core], dst_ref=part_in.at[n, slot],
                send_sem=a_send.at[n], recv_sem=a_recv.at[n], device_id=peer, device_id_type=MESH,
            ).start()

    def start_b(n):
        drain(part_in.at[n, pl.ds(1, 7)], a_recv.at[n])
        total = part[n, core]
        for slot in range(1, 8):
            total += part_in[n, slot]
        half[n] = total
        for i, peer in b_peers:
            pltpu.make_async_remote_copy(
                src_ref=half.at[n], dst_ref=half_in.at[n, i],
                send_sem=b_send.at[n], recv_sem=b_recv.at[n], device_id=peer, device_id_type=MESH,
            ).start()

    def finish_b(n):
        drain(half_in.at[n], b_recv.at[n])
        total = half[n]
        for i in range(15):
            total += half_in[n, i]
        return total

    def share(n, factor):
        factors[n, core] = factor
        pltpu.make_async_remote_copy(
            src_ref=factors.at[n, core], dst_ref=factors.at[n, core],
            send_sem=c_send.at[n], recv_sem=c_recv.at[n], device_id=partner, device_id_type=MESH,
        ).start()
        drain(factors.at[n, 1 - core], c_recv.at[n])
        return factors[n].reshape(32, 128)

    start_a(0, scatter(counts))

    def fill_halo(depth, get, put, row_in, col_in, corner_in):
        east = pltpu.roll(col_in[0], 120, 1)
        west = col_in[1]
        for k in range(1, depth + 1):
            both = jnp.where(q < 4, spread(west[8 - k : 9 - k]), spread(east[k - 1 : k]))
            for r in range(STEP):
                put(r, 15 + k, pltpu.roll(both, (128 - 8 * r) % 128, 1) if r else both)

        def mirrored(j, t, value):
            return jnp.where(mirror_top, get(j - 1, t), jnp.where(mirror_bottom, get(STEP - j, t), value))

        q_wide = lax.broadcasted_iota(I32, (8, COLS), 0)
        for j in range(1, depth + 1):
            wide = jnp.where(
                q_wide < 4,
                spread(row_in[0, 8 - j : 9 - j, :], (8, COLS)),
                spread(row_in[1, j - 1 : j, :], (8, COLS)),
            )
            rows = jnp.concatenate([wide[:, tile(t)] for t in range(TILES)], axis=0)
            for t, value in enumerate(turned(rows, j % 4)):
                put(15 + j, t, mirrored(j, t, value))
        for k in range(1, depth):
            near, far = jnp.full((8, 128), k - 1, I32), jnp.full((8, 128), 128 - k, I32)
            north = jnp.where(lane < 64, pick(corner_in[1], far), pick(corner_in[0], near))
            south = jnp.where(lane < 64, pick(corner_in[3], far), pick(corner_in[2], near))
            for j in range(1, depth + 1 - k):
                value = jnp.where(s < 4, spread(north[8 - j : 9 - j]), spread(south[j - 1 : j]))
                put(15 + j, 15 + k, mirrored(j, 15 + k, value))

    def sweeper(src, dst):
        def get(row, a, b):
            return level[src, row, a:b]

        def vertical(row, a, b):
            if row == 0:
                north = jnp.where(s == 0, get(STEP, a, b), pltpu.roll(get(STEP - 1, a, b), 1, 2))
                return north + get(1, a, b)
            if row == STEP - 1:
                south = jnp.where(s == 7, get(STEP, a, b), pltpu.roll(get(0, a, b), 127, 2))
                return get(STEP - 2, a, b) + south
            if row == STEP:
                return jnp.where(s < 4, get(0, a, b), get(STEP - 1, a, b)) + get(STEP + 1, a, b)
            return get(row - 1, a, b) + get(row + 1, a, b)

        def west_edge(row):
            value = pltpu.roll(level[src, row, STEP - 1], 1, 0)
            return jnp.where(q == 0, jnp.where(lane < 8, level[src, row, STEP], pltpu.roll(value, 8, 1)), value)[None]

        def east_edge(row):
            value = pltpu.roll(level[src, row, 0], 7, 0)
            return jnp.where(q == 7, jnp.where(lane >= 120, level[src, row, STEP], pltpu.roll(value, 120, 1)), value)[None]

        def span(row, a, b):
            lo, hi = max(a - 1, 0), min(b + 1, STEP)
            values = get(row, lo, hi)
            centre = values[a - lo : b - lo]
            west = [values[0 : b - 1 - lo]] if b - 1 > lo else []
            east = [values[a + 1 - lo :]] if a + 1 < hi else []
            west = jnp.concatenate(west if a > 0 else [west_edge(row)] + west, axis=0)
            east = jnp.concatenate(east if b < STEP else east + [east_edge(row)], axis=0)
            level[dst, row, a:b] = (centre + vertical(row, a, b)) + (west + east)

        def beyond(row, count):
            for k in range(1, count + 1):
                if k == 1:
                    inward = jnp.where(q < 4, level[src, row, 0], level[src, row, STEP - 1])[None]
                else:
                    inward = get(row, 14 + k, 15 + k)
                outward = get(row, 16 + k, 17 + k)
                at = (15 + k, 16 + k)
                level[dst, row, at[0] : at[1]] = (get(row, *at) + vertical(row, *at)) + (inward + outward)

        return span, beyond

    def outer_rows(beyond, span, left):
        for row in range(STEP):
            beyond(row, left)
        for j in range(1, left + 1):
            span(15 + j, 0, STEP)
            beyond(15 + j, left - j)

    for n in range(1, SWEEPS + 1):
        span, _ = sweeper(n - 1, n)
        for row in range(n, STEP - n):
            span(row, n, STEP - n)

    def put_prior(row, t, value):
        level[0, row, t] = value

    for ref, m in ((prow, 0), (pcol, 1), (pcorner, 2)):
        drain(ref, halo_recv.at[m])
    fill_halo(DEPTH, lambda row, t: level[0, row, t], put_prior, prow, pcol, pcorner)
    for n in range(1, SWEEPS + 1):
        span, beyond = sweeper(n - 1, n)
        for row in range(STEP):
            if n <= row < STEP - n:
                span(row, 0, n)
                span(row, STEP - n, STEP)
            else:
                span(row, 0, STEP)
        outer_rows(beyond, span, DEPTH - n)

    start_b(0)
    start_a(1, scatter([block_sums(SWEEPS, h) for h in range(2)]))

    def put_ids(row, t, value):
        ids[row, t] = value

    for ref, m in ((zrow, 0), (zcol, 1), (zcorner, 2)):
        drain(ref, zhalo_recv.at[m])
    fill_halo(IDS, lambda row, t: ids[row, t], put_ids, zrow, zcol, zcorner)

    def beside_ids(cells, own_cells):
        other = jnp.full((8, 128), -1, I32)
        for row, t in cells:
            value = ids[row, t]
            other = jnp.maximum(other, jnp.where(value == own_cells, -1, value))
        return jnp.where(lane[0:1] < 64, other[0:1], other[7:8])

    for h in range(2):
        cells = [(row, 15 + k) for row in range(8 * h, 8 * h + 8) for k in range(1, IDS + 1)]
        encode(beside_ids(cells, own[h]), 5 + h)
    lines, cells = own_ids(STEP)
    own.append(cells)
    encode(lines[0], 7)
    encode(lines[1], 8)
    corner = beside_ids([(15 + j, 15 + k) for j in range(1, IDS) for k in range(1, IDS + 1 - j)], own[2])
    encode(corner, 9)

    start_b(1)
    rate_copy.wait()
    target = rate_in[core] * finish_b(0)

    def lookup(table, groups):
        rows = jnp.dot(split2(table), onehot_lo[:, 0 : 128 * groups], preferred_element_type=F32)
        rows = rows[0:32] + rows[32:64]
        lines = []
        for g in range(groups):
            lines.append(spread(jnp.sum(rows[:, 128 * g : 128 * g + 128] * onehot_hi[g], axis=0, keepdims=True)))
        return lines

    def cell_factors(near, far, ext):
        mine = jnp.where(q < 4, near, far)
        next_block = jnp.where(lane >= 120, ext, pltpu.roll(near, 120, 1))
        return mine, jnp.where(q < 4, far, next_block)

    def factors_of(lines):
        ext = lines[4]
        return [cell_factors(lines[0], lines[1], ext), cell_factors(lines[2], lines[3], pltpu.roll(ext, 120, 1))]

    lines = lookup(share(0, target / finish_b(1)), GROUPS)
    pairs = factors_of(lines) + [cell_factors(lines[7], lines[8], lines[9])]
    sides = [lines[5], lines[6], lines[9]]
    for row in range(STEP + IDS):
        h = row // 8
        mine, east = pairs[h]
        scale = jnp.where(ids[row, 0:STEP] == own[h], mine, east)
        level[SWEEPS, row, 0:STEP] = level[SWEEPS, row, 0:STEP] * scale
        left = IDS if row < STEP else IDS - (row - 15)
        if left:
            reach = slice(STEP, STEP + left)
            scale = jnp.where(ids[row, reach] == own[h], mine, sides[h])
            level[SWEEPS, row, reach] = level[SWEEPS, row, reach] * scale

    for n in range(1, SWEEPS + 1):
        span, beyond = sweeper((n + 2) % 4, (n + 3) % 4)
        for row in range(STEP):
            span(row, 0, STEP)
        outer_rows(beyond, span, SWEEPS - n)

    start_a(2, scatter([block_sums(2, h) for h in range(2)]))
    start_b(2)
    pairs = factors_of(lookup(share(1, target / finish_b(2)), 5))
    for r in range(STEP):
        mine, east = pairs[r // 8]
        slot = r % 4
        for t in range(STEP):
            scale = jnp.where(ids[r, t] == own[r // 8], mine, east)
            turn.at[slot][pl.ds(t, 8, stride=STEP), :] = level[2, r, t] * scale
        rows = turn[slot].T
        for t in range(TILES):
            pin.at[t][pl.ds(r, 8, stride=STEP), :] = rows[8 * t : 8 * t + 8]
    for t in range(TILES):
        pltpu.make_async_copy(pin.at[t], out.at[:, tile(t)], store_sem).start()

    for sems, shapes in ((halo_send, (prow, pcol, pcorner)), (zhalo_send, (zrow, zcol, zcorner))):
        for m, ref in enumerate(shapes):
            drain(ref, sems.at[m])
    for n in range(3):
        drain(part_in.at[n, pl.ds(1, 7)], a_send.at[n])
        drain(half_in.at[n], b_send.at[n])
    for n in range(2):
        drain(factors.at[n, core], c_send.at[n])
    drain(pin, store_sem)


def body(prior, zone_ids, rate):
    dma = pltpu.SemaphoreType.DMA
    vmem = pltpu.VMEM
    anywhere = pl.BlockSpec(memory_space=pl.ANY)
    return pl.pallas_call(
        kernel,
        out_shape=jax.ShapeDtypeStruct((ROWS, COLS), F32),
        in_specs=[anywhere, anywhere, anywhere],
        out_specs=anywhere,
        scratch_shapes=[
            vmem((TILES, ROWS, 128), F32),
            vmem((TILES, ROWS, 128), I32),
            vmem((4, 128, 128), F32),
            vmem((4, 128, 128), I32),
            vmem((4, SIDE, SIDE, 8, 128), F32),
            vmem((STEP + IDS, STEP + IDS, 8, 128), I32),
            vmem((2, 8, COLS), F32),
            vmem((2, 8, 128), F32),
            vmem((4, 8, 128), F32),
            vmem((2, 8, COLS), I32),
            vmem((2, 8, 128), I32),
            vmem((4, 8, 128), I32),
            vmem((2, 8, 128), F32),
            vmem((2, 8, 128), I32),
            vmem((GROUPS, 32, 128), F32),
            vmem((128, 128 * GROUPS), BF16),
            vmem((3, 2, 16, 128), F32),
            vmem((3, 8, 16, 128), F32),
            vmem((3, 16, 128), F32),
            vmem((3, 15, 16, 128), F32),
            vmem((2, 2, 16, 128), F32),
            dma((2, 3)),
            dma,
            dma,
            dma((3,)),
            dma((3,)),
            dma((3,)),
            dma((3,)),
            dma((3,)),
            dma((3,)),
            dma((3,)),
            dma((3,)),
            dma((2,)),
            dma((2,)),
            vmem((2, 16, 128), F32),
        ],
        compiler_params=pltpu.CompilerParams(collective_id=0, has_side_effects=True),
    )(prior, zone_ids, rate.reshape(2, 16, 128))


def solution(mesh):
    placed = (P("lat", "lon"), P("lat", "lon"), P())
    return jax.shard_map(
        body, mesh=mesh, in_specs=placed, out_specs=P("lat", "lon"), check_vma=False
    )
```

```python
import jax
import jax.numpy as jnp
from jax import lax
from jax.experimental import pallas as pl
from jax.experimental.pallas import tpu as pltpu
from jax.sharding import PartitionSpec as P

ROWS, COLS = 128, 2048
STEP = 16
TILES = COLS // 128
SWEEPS = 3
DEPTH = 6
IDS = 3
SIDE = STEP + DEPTH
GROUPS = 10
VMEM_LIMIT = 55200000
MESH = pl.DeviceIdType.MESH
F32, I32, BF16 = jnp.float32, jnp.int32, jnp.bfloat16


def split2(x):
    high = x.astype(BF16)
    low = (x - high.astype(F32)).astype(BF16)
    return jnp.concatenate([high, low], axis=0)


def place(row, col):
    return {"lat": jnp.bitwise_and(row, 7), "lon": jnp.bitwise_and(col, 15)}


def device(x, core, y, z):
    return (jnp.bitwise_and(x, 3) * 2 + core, jnp.bitwise_and(y, 3) * 4 + jnp.bitwise_and(z, 3))


FAR_A = [2, 3, 1, 0]
FAR_B = sorted(
    [(a, b) for a in range(4) for b in range(4) if (a, b) != (0, 0)],
    key=lambda t: -(min(t[0], 4 - t[0]) + min(t[1], 4 - t[1])),
)


def drain(ref, sem):
    pltpu.make_async_copy(ref, ref, sem).wait()


def kernel(
    prior, zones, rate, final,
    pin, zin, turn, iturn, level0, level1, level2, level3, ids,
    prow, pcol, pcorner, zrow, zcol, zcorner, ppack, zpack,
    onehot_hi, onehot_lo,
    part, part_in, half, half_in, factors,
    load_sem, rate_sem, halo_send, halo_recv, zhalo_send, zhalo_recv,
    a_send, a_recv, b_send, b_recv, c_send, c_recv, rate_in,
):
    level = [level0, level1, level2, level3]
    lat, lon = lax.axis_index("lat"), lax.axis_index("lon")
    x, core = jnp.right_shift(lat, 1), jnp.bitwise_and(lat, 1)
    y, z = jnp.right_shift(lon, 2), jnp.bitwise_and(lon, 3)

    around = [(-1, 0), (1, 0), (0, -1), (0, 1), (-1, -1), (-1, 1), (1, -1), (1, 1)]
    a_peers = []
    for d in FAR_A:
        for flip in (1, 0):
            if (d, flip) != (0, 0):
                a_peers.append((d * 2 + flip, flip, device(x + d, 1 - core if flip else core, y, z)))
    b_peers = [(i, device(x, core, y + a, z + b)) for i, (a, b) in enumerate(FAR_B)]
    partner = device(x, 1 - core, y, z)

    barrier = pltpu.get_barrier_semaphore()
    greeted = 0
    for dr, dc in around:
        pl.semaphore_signal(barrier, inc=1, device_id=place(lat + dr, lon + dc), device_id_type=MESH)
        greeted += 1

    def tile(t):
        return slice(128 * t, 128 * t + 128)

    for n, t in [(0, 0), (0, TILES - 1), (1, 0), (1, TILES - 1)] + [(n, t) for n in (0, 1) for t in range(1, TILES - 1)]:
        sem = load_sem.at[n, 0 if t == 0 else 1 if t == TILES - 1 else 2]
        pltpu.make_async_copy((prior, zones)[n].at[:, tile(t)], (pin, zin)[n].at[t], sem).start()
    rate_copy = pltpu.make_async_copy(rate, rate_in, rate_sem)
    rate_copy.start()

    for _, _, peer in a_peers:
        pl.semaphore_signal(barrier, inc=1, device_id=peer, device_id_type=MESH)
        greeted += 1
    for _, peer in b_peers:
        pl.semaphore_signal(barrier, inc=1, device_id=peer, device_id_type=MESH)
        greeted += 1

    lane = lax.broadcasted_iota(I32, (8, 128), 1)
    q = lax.broadcasted_iota(I32, (8, 128), 0)
    s = lax.rem(lane, 8)
    mirror_top = s + 8 * lat < 4
    mirror_bottom = s + 8 * lat >= 60

    def pick(value, index):
        return jnp.take_along_axis(value, index, axis=1, mode="promise_in_bounds")

    def spread(row, shape=(8, 128)):
        return jnp.broadcast_to(row, shape)

    def pack(ref, packed):
        index = 16 * s + lax.div(lane, 8)
        packed[0] = pick(ref[0].T[0:8], index)
        packed[1] = pick(ref[TILES - 1].T[120:128], index)

    first8, last8 = pl.ds(0, 8), pl.ds(ROWS - 8, 8)
    first128, last128 = pl.ds(0, 128), pl.ds(COLS - 128, 128)

    def send(src, dst, send_sem, recv_sem, dr, dc):
        pltpu.make_async_remote_copy(
            src_ref=src, dst_ref=dst, send_sem=send_sem, recv_sem=recv_sem,
            device_id=place(lat + dr, lon + dc), device_id_type=MESH,
        ).start()

    def send_rows(source, row_in, corner_in, out_sem, in_sem):
        send(source.at[first8, first128], corner_in.at[2], out_sem.at[2], in_sem.at[2], -1, -1)
        send(source.at[first8, last128], corner_in.at[3], out_sem.at[2], in_sem.at[2], -1, 1)
        send(source.at[last8, first128], corner_in.at[0], out_sem.at[2], in_sem.at[2], 1, -1)
        send(source.at[last8, last128], corner_in.at[1], out_sem.at[2], in_sem.at[2], 1, 1)
        send(source.at[first8, :], row_in.at[1], out_sem.at[0], in_sem.at[0], -1, 0)
        send(source.at[last8, :], row_in.at[0], out_sem.at[0], in_sem.at[0], 1, 0)

    def send_cols(packed, col_in, out_sem, in_sem):
        send(packed.at[0], col_in.at[0], out_sem.at[1], in_sem.at[1], 0, -1)
        send(packed.at[1], col_in.at[1], out_sem.at[1], in_sem.at[1], 0, 1)

    pl.semaphore_wait(barrier, greeted)
    send_rows(prior, prow, pcorner, halo_send, halo_recv)
    drain(pin.at[0], load_sem.at[0, 0])
    drain(pin.at[TILES - 1], load_sem.at[0, 1])
    pack(pin, ppack)
    send_cols(ppack, pcol, halo_send, halo_recv)
    drain(zin.at[0], load_sem.at[1, 0])
    drain(zin.at[TILES - 1], load_sem.at[1, 1])
    pack(zin, zpack)
    send_cols(zpack, zcol, zhalo_send, zhalo_recv)
    send_rows(zones, zrow, zcorner, zhalo_send, zhalo_recv)

    inner = pl.ds(1, TILES - 2)

    def turned(matrix, slot):
        buffer = turn if matrix.dtype == F32 else iturn
        buffer[slot] = matrix.T
        return [buffer.at[slot][pl.ds(t, 8, stride=STEP), :] for t in range(STEP)]

    def load_planes(ref, write):
        for r in range(STEP):
            rows = [ref.at[t][pl.ds(r, 8, stride=STEP), :] for t in range(TILES)]
            for t, value in enumerate(turned(jnp.concatenate(rows, axis=0), r % 4)):
                write(r, t, value)

    def write_prior(r, t, value):
        level0[r, t] = value

    def write_ids(r, t, value):
        ids[r, t] = value

    drain(pin.at[inner], load_sem.at[0, 2])
    load_planes(pin, write_prior)
    drain(zin.at[inner], load_sem.at[1, 2])
    load_planes(zin, write_ids)

    hi_iota = lax.broadcasted_iota(I32, (32, 128), 0)
    lo_iota = lax.broadcasted_iota(I32, (128, 128), 0)

    def encode(line, group):
        hi = jnp.right_shift(line, 7)
        lo = jnp.bitwise_and(line, 127)
        onehot_hi[group] = jnp.where(hi_iota == hi, 1.0, 0.0)
        onehot_lo[:, 128 * group : 128 * group + 128] = jnp.where(lo_iota == lo, 1.0, 0.0).astype(BF16)

    def own_ids(row):
        value = ids[row, 0]
        return [value[0:1], value[4:5]], jnp.where(q < 4, spread(value[0:1]), spread(value[4:5]))

    own = []
    for h in range(2):
        lines, cells = own_ids(8 * h)
        own.append(cells)
        for g in range(2):
            encode(lines[g], 2 * h + g)

    def fold(value):
        value = value + pltpu.roll(value, 7, 0)
        value = value + pltpu.roll(value, 6, 0)
        return value[0:1], value[4:5]

    def scatter(pairs):
        lines, ext = [], []
        for own_sum, east_sum in pairs:
            own0, own1 = fold(own_sum)
            east0, east1 = fold(east_sum)
            east1 = spread(east1)
            beyond = pltpu.roll(east1, 8, 1)[0:1]
            lines.append(own0 + jnp.where(lane[0:1] >= 8, beyond, 0.0))
            lines.append(own1 + east0)
            ext.append((east1[0:1], beyond))
        lines.append(jnp.where(lane[0:1] >= 120, ext[0][0], jnp.where(lane[0:1] < 8, ext[1][1], 0.0)))
        weighted = split2(jnp.concatenate([onehot_hi[g] * lines[g] for g in range(5)], axis=1))
        table = lax.dot_general(
            weighted, onehot_lo[:, 0:640], (((1,), (1,)), ((), ())), preferred_element_type=F32
        )
        return table[0:32] + table[32:64]

    def block_sums(source, h):
        own_sum, east_sum = jnp.zeros((STEP, 8, 128), F32), jnp.zeros((STEP, 8, 128), F32)
        for r in range(8 * h, 8 * h + 8):
            matched = ids[r, 0:STEP] == own[h]
            value = source[r, 0:STEP]
            own_sum += jnp.where(matched, value, 0.0)
            east_sum += jnp.where(matched, 0.0, value)
        return jnp.sum(own_sum, axis=0), jnp.sum(east_sum, axis=0)

    counts, others = [], []
    for h in range(2):
        own_sum = jnp.zeros((STEP, 8, 128), F32)
        other = jnp.full((STEP, 8, 128), -1, I32)
        for r in range(8 * h, 8 * h + 8):
            value = ids[r, 0:STEP]
            matched = value == own[h]
            own_sum += jnp.where(matched, 1.0, 0.0)
            other = jnp.maximum(other, jnp.where(matched, -1, value))
        own_sum = jnp.sum(own_sum, axis=0)
        counts.append((own_sum, float(8 * STEP) - own_sum))
        others.append(spread(jnp.max(other, axis=0)[7:8]))
    encode(jnp.where(lane >= 120, others[0], jnp.where(lane < 8, pltpu.roll(others[1], 8, 1), -1))[0:1], 4)

    def start_a(n, table):
        part[n] = table.reshape(2, 16, 128)
        for slot, flip, peer in a_peers:
            pltpu.make_async_remote_copy(
                src_ref=part.at[n, 1 - core if flip else core], dst_ref=part_in.at[n, slot],
                send_sem=a_send.at[n], recv_sem=a_recv.at[n], device_id=peer, device_id_type=MESH,
            ).start()

    def start_b(n):
        drain(part_in.at[n, pl.ds(1, 7)], a_recv.at[n])
        total = part[n, core]
        for slot in range(1, 8):
            total += part_in[n, slot]
        half[n] = total
        for i, peer in b_peers:
            pltpu.make_async_remote_copy(
                src_ref=half.at[n], dst_ref=half_in.at[n, i],
                send_sem=b_send.at[n], recv_sem=b_recv.at[n], device_id=peer, device_id_type=MESH,
            ).start()

    def finish_b(n):
        drain(half_in.at[n], b_recv.at[n])
        total = half[n]
        for i in range(15):
            total += half_in[n, i]
        return total

    def share(n, factor):
        factors[n, core] = factor
        pltpu.make_async_remote_copy(
            src_ref=factors.at[n, core], dst_ref=factors.at[n, core],
            send_sem=c_send.at[n], recv_sem=c_recv.at[n], device_id=partner, device_id_type=MESH,
        ).start()
        drain(factors.at[n, 1 - core], c_recv.at[n])
        return factors[n].reshape(32, 128)

    start_a(0, scatter(counts))

    def fill_halo(depth, get, put, row_in, col_in, corner_in, sems):
        def mirrored(j, t, value):
            return jnp.where(mirror_top, get(j - 1, t), jnp.where(mirror_bottom, get(STEP - j, t), value))

        drain(col_in, sems.at[1])
        east = pltpu.roll(col_in[0], 120, 1)
        west = col_in[1]
        for k in range(1, depth + 1):
            both = jnp.where(q < 4, spread(west[8 - k : 9 - k]), spread(east[k - 1 : k]))
            for r in range(STEP):
                put(r, 15 + k, pltpu.roll(both, (128 - 8 * r) % 128, 1) if r else both)
        drain(corner_in, sems.at[2])
        for k in range(1, depth):
            near, far = jnp.full((8, 128), k - 1, I32), jnp.full((8, 128), 128 - k, I32)
            north = jnp.where(lane < 64, pick(corner_in[1], far), pick(corner_in[0], near))
            south = jnp.where(lane < 64, pick(corner_in[3], far), pick(corner_in[2], near))
            for j in range(1, depth + 1 - k):
                value = jnp.where(s < 4, spread(north[8 - j : 9 - j]), spread(south[j - 1 : j]))
                put(15 + j, 15 + k, mirrored(j, 15 + k, value))
        drain(row_in, sems.at[0])
        q_wide = lax.broadcasted_iota(I32, (8, COLS), 0)
        for j in range(1, depth + 1):
            wide = jnp.where(
                q_wide < 4,
                spread(row_in[0, 8 - j : 9 - j, :], (8, COLS)),
                spread(row_in[1, j - 1 : j, :], (8, COLS)),
            )
            rows = jnp.concatenate([wide[:, tile(t)] for t in range(TILES)], axis=0)
            for t, value in enumerate(turned(rows, j % 4)):
                put(15 + j, t, mirrored(j, t, value))

    def sweeper(src, dst):
        def get(row, a, b):
            return src[row, a:b]

        def vertical(row, a, b):
            if row == 0:
                north = jnp.where(s == 0, get(STEP, a, b), pltpu.roll(get(STEP - 1, a, b), 1, 2))
                return north + get(1, a, b)
            if row == STEP - 1:
                south = jnp.where(s == 7, get(STEP, a, b), pltpu.roll(get(0, a, b), 127, 2))
                return get(STEP - 2, a, b) + south
            if row == STEP:
                return jnp.where(s < 4, get(0, a, b), get(STEP - 1, a, b)) + get(STEP + 1, a, b)
            return get(row - 1, a, b) + get(row + 1, a, b)

        def west_edge(row):
            value = pltpu.roll(src[row, STEP - 1], 1, 0)
            return jnp.where(q == 0, jnp.where(lane < 8, src[row, STEP], pltpu.roll(value, 8, 1)), value)[None]

        def east_edge(row):
            value = pltpu.roll(src[row, 0], 7, 0)
            return jnp.where(q == 7, jnp.where(lane >= 120, src[row, STEP], pltpu.roll(value, 120, 1)), value)[None]

        def span(row, a, b):
            lo, hi = max(a - 1, 0), min(b + 1, STEP)
            values = get(row, lo, hi)
            centre = values[a - lo : b - lo]
            west = [values[0 : b - 1 - lo]] if b - 1 > lo else []
            east = [values[a + 1 - lo :]] if a + 1 < hi else []
            west = jnp.concatenate(west if a > 0 else [west_edge(row)] + west, axis=0)
            east = jnp.concatenate(east if b < STEP else east + [east_edge(row)], axis=0)
            dst[row, a:b] = (centre + vertical(row, a, b)) + (west + east)

        def beyond(row, count):
            for k in range(1, count + 1):
                if k == 1:
                    inward = jnp.where(q < 4, src[row, 0], src[row, STEP - 1])[None]
                else:
                    inward = get(row, 14 + k, 15 + k)
                outward = get(row, 16 + k, 17 + k)
                at = (15 + k, 16 + k)
                dst[row, at[0] : at[1]] = (get(row, *at) + vertical(row, *at)) + (inward + outward)

        return span, beyond

    def outer_rows(beyond, span, left):
        for row in range(STEP):
            beyond(row, left)
        for j in range(1, left + 1):
            span(15 + j, 0, STEP)
            beyond(15 + j, left - j)

    for n in range(1, SWEEPS + 1):
        span, _ = sweeper(level[n - 1], level[n])
        for row in range(n, STEP - n):
            span(row, n, STEP - n)

    def put_prior(row, t, value):
        level0[row, t] = value

    fill_halo(DEPTH, lambda row, t: level0[row, t], put_prior, prow, pcol, pcorner, halo_recv)
    for n in range(1, SWEEPS + 1):
        span, beyond = sweeper(level[n - 1], level[n])
        for row in range(STEP):
            if n <= row < STEP - n:
                span(row, 0, n)
                span(row, STEP - n, STEP)
            else:
                span(row, 0, STEP)
        outer_rows(beyond, span, DEPTH - n)

    start_a(1, scatter([block_sums(level3, h) for h in range(2)]))
    start_b(0)

    def put_ids(row, t, value):
        ids[row, t] = value

    fill_halo(IDS, lambda row, t: ids[row, t], put_ids, zrow, zcol, zcorner, zhalo_recv)

    def beside_ids(cells, own_cells):
        other = jnp.full((8, 128), -1, I32)
        for row, t in cells:
            value = ids[row, t]
            other = jnp.maximum(other, jnp.where(value == own_cells, -1, value))
        return jnp.where(lane[0:1] < 64, other[0:1], other[7:8])

    for h in range(2):
        cells = [(row, 15 + k) for row in range(8 * h, 8 * h + 8) for k in range(1, IDS + 1)]
        encode(beside_ids(cells, own[h]), 5 + h)
    lines, cells = own_ids(STEP)
    own.append(cells)
    encode(lines[0], 7)
    encode(lines[1], 8)
    corner = beside_ids([(15 + j, 15 + k) for j in range(1, IDS) for k in range(1, IDS + 1 - j)], own[2])
    encode(corner, 9)

    start_b(1)
    rate_copy.wait()
    target = rate_in[core] * finish_b(0)

    def lookup(table, groups):
        rows = jnp.dot(split2(table), onehot_lo[:, 0 : 128 * groups], preferred_element_type=F32)
        rows = rows[0:32] + rows[32:64]
        lines = []
        for g in range(groups):
            lines.append(spread(jnp.sum(rows[:, 128 * g : 128 * g + 128] * onehot_hi[g], axis=0, keepdims=True)))
        return lines

    def cell_factors(near, far, ext):
        mine = jnp.where(q < 4, near, far)
        next_block = jnp.where(lane >= 120, ext, pltpu.roll(near, 120, 1))
        return mine, jnp.where(q < 4, far, next_block)

    def factors_of(lines):
        ext = lines[4]
        return [cell_factors(lines[0], lines[1], ext), cell_factors(lines[2], lines[3], pltpu.roll(ext, 120, 1))]

    lines = lookup(share(0, target / finish_b(1)), GROUPS)
    pairs = factors_of(lines) + [cell_factors(lines[7], lines[8], lines[9])]
    sides = [lines[5], lines[6], lines[9]]
    for row in range(STEP + IDS):
        h = row // 8
        mine, east = pairs[h]
        scale = jnp.where(ids[row, 0:STEP] == own[h], mine, east)
        level3[row, 0:STEP] = level3[row, 0:STEP] * scale
        left = IDS if row < STEP else IDS - (row - 15)
        if left:
            reach = slice(STEP, STEP + left)
            scale = jnp.where(ids[row, reach] == own[h], mine, sides[h])
            level3[row, reach] = level3[row, reach] * scale

    for n in range(1, SWEEPS + 1):
        span, beyond = sweeper(level[(n + 2) % 4], level[n - 1] if n < SWEEPS else final)
        for row in range(STEP):
            span(row, 0, STEP)
        outer_rows(beyond, span, SWEEPS - n)

    start_a(2, scatter([block_sums(final, h) for h in range(2)]))
    start_b(2)
    pairs = factors_of(lookup(share(1, target / finish_b(2)), 5))
    for r in range(STEP):
        mine, east = pairs[r // 8]
        final[r] = final[r] * jnp.where(ids[r, 0:STEP] == own[r // 8], mine, east)

    for sems, shapes in ((halo_send, (prow, pcol, pcorner)), (zhalo_send, (zrow, zcol, zcorner))):
        for m, ref in enumerate(shapes):
            drain(ref, sems.at[m])
    for n in range(3):
        drain(part_in.at[n, pl.ds(1, 7)], a_send.at[n])
        drain(half_in.at[n], b_send.at[n])
    for n in range(2):
        drain(factors.at[n, core], c_send.at[n])


def finish(final, out, turn, pout, store_sem):
    for h in range(2):
        for r in range(8 * h, 8 * h + 8):
            slot = r % 4
            for t in range(STEP):
                turn.at[slot][pl.ds(t, 8, stride=STEP), :] = final[r, t]
            rows = turn[slot].T
            for t in range(TILES):
                pout.at[t][pl.ds(r, 8, stride=STEP), :] = rows[8 * t : 8 * t + 8]
        for t in range(TILES):
            pltpu.make_async_copy(
                pout.at[t].reshape(8, STEP, 128).at[:, 8 * h : 8 * h + 8, :],
                out.reshape(8, STEP, COLS).at[:, 8 * h : 8 * h + 8, 128 * t : 128 * t + 128],
                store_sem,
            ).start()
    drain(pout, store_sem)


def body(prior, zone_ids, rate):
    dma = pltpu.SemaphoreType.DMA
    vmem = pltpu.VMEM
    outside = pl.BlockSpec(memory_space=pltpu.HBM)
    inside = pl.BlockSpec(memory_space=pltpu.VMEM)
    scaled = pl.pallas_call(
        kernel,
        out_shape=jax.ShapeDtypeStruct((STEP, STEP, 8, 128), F32),
        in_specs=[outside] * 3,
        out_specs=inside,
        scratch_shapes=[
            vmem((TILES, ROWS, 128), F32),
            vmem((TILES, ROWS, 128), I32),
            vmem((4, 128, 128), F32),
            vmem((4, 128, 128), I32),
            vmem((SIDE, SIDE, 8, 128), F32),
            vmem((SIDE, SIDE, 8, 128), F32),
            vmem((SIDE, SIDE, 8, 128), F32),
            vmem((SIDE, SIDE, 8, 128), F32),
            vmem((STEP + IDS, STEP + IDS, 8, 128), I32),
            vmem((2, 8, COLS), F32),
            vmem((2, 8, 128), F32),
            vmem((4, 8, 128), F32),
            vmem((2, 8, COLS), I32),
            vmem((2, 8, 128), I32),
            vmem((4, 8, 128), I32),
            vmem((2, 8, 128), F32),
            vmem((2, 8, 128), I32),
            vmem((GROUPS, 32, 128), F32),
            vmem((128, 128 * GROUPS), BF16),
            vmem((3, 2, 16, 128), F32),
            vmem((3, 8, 16, 128), F32),
            vmem((3, 16, 128), F32),
            vmem((3, 15, 16, 128), F32),
            vmem((2, 2, 16, 128), F32),
            dma((2, 3)),
            dma,
            dma((3,)),
            dma((3,)),
            dma((3,)),
            dma((3,)),
            dma((3,)),
            dma((3,)),
            dma((3,)),
            dma((3,)),
            dma((2,)),
            dma((2,)),
            vmem((2, 16, 128), F32),
        ],
        compiler_params=pltpu.CompilerParams(
            collective_id=0, has_side_effects=True, vmem_limit_bytes=VMEM_LIMIT
        ),
    )(prior, zone_ids, rate.reshape(2, 16, 128))
    return pl.pallas_call(
        finish,
        out_shape=jax.ShapeDtypeStruct((ROWS, COLS), F32),
        in_specs=[inside],
        out_specs=outside,
        scratch_shapes=[vmem((4, 128, 128), F32), vmem((TILES, ROWS, 128), F32), dma],
        compiler_params=pltpu.CompilerParams(vmem_limit_bytes=32 * 1024 * 1024),
    )(scaled)


def solution(mesh):
    placed = (P("lat", "lon"), P("lat", "lon"), P())
    return jax.shard_map(
        body, mesh=mesh, in_specs=placed, out_specs=P("lat", "lon"), check_vma=False
    )
```

```python
import jax
import jax.numpy as jnp
from jax import lax
from jax.experimental import pallas as pl
from jax.experimental.pallas import tpu as pltpu
from jax.sharding import PartitionSpec as P

ROWS, COLS = 128, 2048
STEP = 16
TILES = COLS // 128
SWEEPS = 3
DEPTH = 6
IDS = 3
SIDE = STEP + DEPTH
GROUPS = 10
VMEM_LIMIT = 55200000
MESH = pl.DeviceIdType.MESH
F32, I32, BF16 = jnp.float32, jnp.int32, jnp.bfloat16


def split2(x):
    high = x.astype(BF16)
    low = (x - high.astype(F32)).astype(BF16)
    return jnp.concatenate([high, low], axis=0)


def place(row, col):
    return {"lat": jnp.bitwise_and(row, 7), "lon": jnp.bitwise_and(col, 15)}


def device(x, core, y, z):
    return (jnp.bitwise_and(x, 3) * 2 + core, jnp.bitwise_and(y, 3) * 4 + jnp.bitwise_and(z, 3))


FAR_A = [2, 3, 1, 0]
FAR_B = sorted(
    [(a, b) for a in range(4) for b in range(4) if (a, b) != (0, 0)],
    key=lambda t: -(min(t[0], 4 - t[0]) + min(t[1], 4 - t[1])),
)


def drain(ref, sem):
    pltpu.make_async_copy(ref, ref, sem).wait()


def kernel(
    prior, zones, rate, signed, scales,
    pin, zin, turn, iturn, level0, level1, level2, level3, final, ids,
    prow, pcol, pcorner, zrow, zcol, zcorner, ppack, zpack,
    onehot_hi, onehot_lo,
    part, part_in, half, half_in, factors,
    load_sem, rate_sem, halo_send, halo_recv, zhalo_send, zhalo_recv,
    a_send, a_recv, b_send, b_recv, c_send, c_recv, rate_in,
):
    level = [level0, level1, level2, level3]
    lat, lon = lax.axis_index("lat"), lax.axis_index("lon")
    x, core = jnp.right_shift(lat, 1), jnp.bitwise_and(lat, 1)
    y, z = jnp.right_shift(lon, 2), jnp.bitwise_and(lon, 3)

    around = [(-1, 0), (1, 0), (0, -1), (0, 1), (-1, -1), (-1, 1), (1, -1), (1, 1)]
    a_peers = []
    for d in FAR_A:
        for flip in (1, 0):
            if (d, flip) != (0, 0):
                a_peers.append((d * 2 + flip, flip, device(x + d, 1 - core if flip else core, y, z)))
    b_peers = [(i, device(x, core, y + a, z + b)) for i, (a, b) in enumerate(FAR_B)]
    partner = device(x, 1 - core, y, z)

    barrier = pltpu.get_barrier_semaphore()
    greeted = 0
    for peer in [peer for _, peer in b_peers] + [peer for _, _, peer in a_peers] + [place(lat + dr, lon + dc) for dr, dc in around]:
        pl.semaphore_signal(barrier, inc=1, device_id=peer, device_id_type=MESH)
        greeted += 1

    def tile(t):
        return slice(128 * t, 128 * t + 128)

    for n, t in [(0, 0), (0, TILES - 1), (1, 0), (1, TILES - 1)] + [(n, t) for n in (0, 1) for t in range(1, TILES - 1)]:
        sem = load_sem.at[n, 0 if t == 0 else 1 if t == TILES - 1 else 2]
        pltpu.make_async_copy((prior, zones)[n].at[:, tile(t)], (pin, zin)[n].at[t], sem).start()
    rate_copy = pltpu.make_async_copy(rate, rate_in, rate_sem)
    rate_copy.start()

    lane = lax.broadcasted_iota(I32, (8, 128), 1)
    q = lax.broadcasted_iota(I32, (8, 128), 0)
    s = lax.rem(lane, 8)
    mirror_top = s + 8 * lat < 4
    mirror_bottom = s + 8 * lat >= 60

    def pick(value, index):
        return jnp.take_along_axis(value, index, axis=1, mode="promise_in_bounds")

    def spread(row, shape=(8, 128)):
        return jnp.broadcast_to(row, shape)

    inner = pl.ds(1, TILES - 2)

    def pack(ref, packed):
        index = 16 * s + lax.div(lane, 8)
        packed[0] = pick(ref[0].T[0:8], index)
        packed[1] = pick(ref[TILES - 1].T[120:128], index)

    first8, last8 = pl.ds(0, 8), pl.ds(ROWS - 8, 8)

    def send(src, dst, send_sem, recv_sem, dr, dc):
        pltpu.make_async_remote_copy(
            src_ref=src, dst_ref=dst, send_sem=send_sem, recv_sem=recv_sem,
            device_id=place(lat + dr, lon + dc), device_id_type=MESH,
        ).start()

    def send_rows(source, row_in, corner_in, out_sem, in_sem):
        send(source.at[:, first8, :], row_in.at[1], out_sem.at[0], in_sem.at[0], -1, 0)
        send(source.at[:, last8, :], row_in.at[0], out_sem.at[0], in_sem.at[0], 1, 0)
        send(source.at[0, first8, :], corner_in.at[2], out_sem.at[2], in_sem.at[2], -1, -1)
        send(source.at[TILES - 1, first8, :], corner_in.at[3], out_sem.at[2], in_sem.at[2], -1, 1)
        send(source.at[0, last8, :], corner_in.at[0], out_sem.at[2], in_sem.at[2], 1, -1)
        send(source.at[TILES - 1, last8, :], corner_in.at[1], out_sem.at[2], in_sem.at[2], 1, 1)

    def send_cols(packed, col_in, out_sem, in_sem):
        send(packed.at[0], col_in.at[0], out_sem.at[1], in_sem.at[1], 0, -1)
        send(packed.at[1], col_in.at[1], out_sem.at[1], in_sem.at[1], 0, 1)

    drain(pin.at[0], load_sem.at[0, 0])
    drain(pin.at[TILES - 1], load_sem.at[0, 1])
    pack(pin, ppack)
    drain(pin.at[inner], load_sem.at[0, 2])
    pl.semaphore_wait(barrier, greeted)
    send_rows(pin, prow, pcorner, halo_send, halo_recv)
    send_cols(ppack, pcol, halo_send, halo_recv)

    def turned(matrix, slot):
        buffer = turn if matrix.dtype == F32 else iturn
        buffer[slot] = matrix.T
        return [buffer.at[slot][pl.ds(t, 8, stride=STEP), :] for t in range(STEP)]

    def load_planes(ref, write):
        for r in range(STEP):
            rows = [ref.at[t][pl.ds(r, 8, stride=STEP), :] for t in range(TILES)]
            for t, value in enumerate(turned(jnp.concatenate(rows, axis=0), r % 4)):
                write(r, t, value)

    def write_prior(r, t, value):
        level0[r, t] = value

    def write_ids(r, t, value):
        ids[r, t] = value

    load_planes(pin, write_prior)
    drain(zin.at[0], load_sem.at[1, 0])
    drain(zin.at[TILES - 1], load_sem.at[1, 1])
    pack(zin, zpack)
    drain(zin.at[inner], load_sem.at[1, 2])
    send_cols(zpack, zcol, zhalo_send, zhalo_recv)
    send_rows(zin, zrow, zcorner, zhalo_send, zhalo_recv)
    load_planes(zin, write_ids)

    hi_iota = lax.broadcasted_iota(I32, (32, 128), 0)
    lo_iota = lax.broadcasted_iota(I32, (128, 128), 0)

    def encode(line, group):
        hi = jnp.right_shift(line, 7)
        lo = jnp.bitwise_and(line, 127)
        onehot_hi[group] = jnp.where(hi_iota == hi, 1.0, 0.0)
        onehot_lo[:, 128 * group : 128 * group + 128] = jnp.where(lo_iota == lo, 1.0, 0.0).astype(BF16)

    def own_ids(row):
        value = ids[row, 0]
        return [value[0:1], value[4:5]], jnp.where(q < 4, spread(value[0:1]), spread(value[4:5]))

    own = []
    for h in range(2):
        lines, cells = own_ids(8 * h)
        own.append(cells)
        for g in range(2):
            encode(lines[g], 2 * h + g)

    def fold(value):
        value = value + pltpu.roll(value, 7, 0)
        value = value + pltpu.roll(value, 6, 0)
        return value[0:1], value[4:5]

    def scatter(pairs):
        lines, ext = [], []
        for own_sum, east_sum in pairs:
            own0, own1 = fold(own_sum)
            east0, east1 = fold(east_sum)
            east1 = spread(east1)
            beyond = pltpu.roll(east1, 8, 1)[0:1]
            lines.append(own0 + jnp.where(lane[0:1] >= 8, beyond, 0.0))
            lines.append(own1 + east0)
            ext.append((east1[0:1], beyond))
        lines.append(jnp.where(lane[0:1] >= 120, ext[0][0], jnp.where(lane[0:1] < 8, ext[1][1], 0.0)))
        weighted = split2(jnp.concatenate([onehot_hi[g] * lines[g] for g in range(5)], axis=1))
        table = lax.dot_general(
            weighted, onehot_lo[:, 0:640], (((1,), (1,)), ((), ())), preferred_element_type=F32
        )
        return table[0:32] + table[32:64]

    def block_sums(source, h):
        own_sum, east_sum = jnp.zeros((STEP, 8, 128), F32), jnp.zeros((STEP, 8, 128), F32)
        for r in range(8 * h, 8 * h + 8):
            matched = ids[r, 0:STEP] == own[h]
            value = source[r, 0:STEP]
            own_sum += jnp.where(matched, value, 0.0)
            east_sum += jnp.where(matched, 0.0, value)
        return jnp.sum(own_sum, axis=0), jnp.sum(east_sum, axis=0)

    counts, others = [], []
    for h in range(2):
        own_sum = jnp.zeros((STEP, 8, 128), F32)
        other = jnp.full((STEP, 8, 128), -1, I32)
        for r in range(8 * h, 8 * h + 8):
            value = ids[r, 0:STEP]
            matched = value == own[h]
            own_sum += jnp.where(matched, 1.0, 0.0)
            other = jnp.maximum(other, jnp.where(matched, -1, value))
        own_sum = jnp.sum(own_sum, axis=0)
        counts.append((own_sum, float(8 * STEP) - own_sum))
        others.append(spread(jnp.max(other, axis=0)[7:8]))
    encode(jnp.where(lane >= 120, others[0], jnp.where(lane < 8, pltpu.roll(others[1], 8, 1), -1))[0:1], 4)

    def start_a(n, table):
        part[n] = table.reshape(2, 16, 128)
        for slot, flip, peer in a_peers:
            pltpu.make_async_remote_copy(
                src_ref=part.at[n, 1 - core if flip else core], dst_ref=part_in.at[n, slot],
                send_sem=a_send.at[n], recv_sem=a_recv.at[n], device_id=peer, device_id_type=MESH,
            ).start()

    def start_b(n):
        drain(part_in.at[n, pl.ds(1, 7)], a_recv.at[n])
        total = part[n, core]
        for slot in range(1, 8):
            total += part_in[n, slot]
        half[n] = total
        for i, peer in b_peers:
            pltpu.make_async_remote_copy(
                src_ref=half.at[n], dst_ref=half_in.at[n, i],
                send_sem=b_send.at[n], recv_sem=b_recv.at[n], device_id=peer, device_id_type=MESH,
            ).start()

    def finish_b(n):
        drain(half_in.at[n], b_recv.at[n])
        total = half[n]
        for i in range(15):
            total += half_in[n, i]
        return total

    def share(n, factor):
        factors[n, core] = factor
        pltpu.make_async_remote_copy(
            src_ref=factors.at[n, core], dst_ref=factors.at[n, core],
            send_sem=c_send.at[n], recv_sem=c_recv.at[n], device_id=partner, device_id_type=MESH,
        ).start()
        drain(factors.at[n, 1 - core], c_recv.at[n])
        return factors[n].reshape(32, 128)

    start_a(0, scatter(counts))

    def fill_sides(depth, put, col_in, sem):
        drain(col_in, sem)
        east = pltpu.roll(col_in[0], 120, 1)
        west = col_in[1]
        for k in range(1, depth + 1):
            both = jnp.where(q < 4, spread(west[8 - k : 9 - k]), spread(east[k - 1 : k]))
            for r in range(STEP):
                put(r, 15 + k, pltpu.roll(both, (128 - 8 * r) % 128, 1) if r else both)

    def fill_ends(depth, get, put, row_in, corner_in, sems):
        def mirrored(j, t, value):
            return jnp.where(mirror_top, get(j - 1, t), jnp.where(mirror_bottom, get(STEP - j, t), value))

        drain(corner_in, sems.at[2])
        for k in range(1, depth):
            near, far = jnp.full((8, 128), k - 1, I32), jnp.full((8, 128), 128 - k, I32)
            north = jnp.where(lane < 64, pick(corner_in[1], far), pick(corner_in[0], near))
            south = jnp.where(lane < 64, pick(corner_in[3], far), pick(corner_in[2], near))
            for j in range(1, depth + 1 - k):
                value = jnp.where(s < 4, spread(north[8 - j : 9 - j]), spread(south[j - 1 : j]))
                put(15 + j, 15 + k, mirrored(j, 15 + k, value))
        drain(row_in, sems.at[0])
        for j in range(1, depth + 1):
            rows = []
            for t in range(TILES):
                north, south = row_in[0, t, 8 - j : 9 - j, :], row_in[1, t, j - 1 : j, :]
                rows.append(jnp.where(q < 4, spread(north), spread(south)))
            for t, value in enumerate(turned(jnp.concatenate(rows, axis=0), j % 4)):
                put(15 + j, t, mirrored(j, t, value))

    def sweeper(src, dst):
        def get(row, a, b):
            return src[row, a:b]

        def vertical(row, a, b):
            if row == 0:
                north = jnp.where(s == 0, get(STEP, a, b), pltpu.roll(get(STEP - 1, a, b), 1, 2))
                return north + get(1, a, b)
            if row == STEP - 1:
                south = jnp.where(s == 7, get(STEP, a, b), pltpu.roll(get(0, a, b), 127, 2))
                return get(STEP - 2, a, b) + south
            if row == STEP:
                return jnp.where(s < 4, get(0, a, b), get(STEP - 1, a, b)) + get(STEP + 1, a, b)
            return get(row - 1, a, b) + get(row + 1, a, b)

        def west_edge(row):
            value = pltpu.roll(src[row, STEP - 1], 1, 0)
            return jnp.where(q == 0, jnp.where(lane < 8, src[row, STEP], pltpu.roll(value, 8, 1)), value)[None]

        def east_edge(row):
            value = pltpu.roll(src[row, 0], 7, 0)
            return jnp.where(q == 7, jnp.where(lane >= 120, src[row, STEP], pltpu.roll(value, 120, 1)), value)[None]

        def span(row, a, b):
            lo, hi = max(a - 1, 0), min(b + 1, STEP)
            values = get(row, lo, hi)
            centre = values[a - lo : b - lo]
            west = [values[0 : b - 1 - lo]] if b - 1 > lo else []
            east = [values[a + 1 - lo :]] if a + 1 < hi else []
            west = jnp.concatenate(west if a > 0 else [west_edge(row)] + west, axis=0)
            east = jnp.concatenate(east if b < STEP else east + [east_edge(row)], axis=0)
            dst[row, a:b] = (centre + vertical(row, a, b)) + (west + east)

        def beyond(row, count):
            for k in range(1, count + 1):
                if k == 1:
                    inward = jnp.where(q < 4, src[row, 0], src[row, STEP - 1])[None]
                else:
                    inward = get(row, 14 + k, 15 + k)
                outward = get(row, 16 + k, 17 + k)
                at = (15 + k, 16 + k)
                dst[row, at[0] : at[1]] = (get(row, *at) + vertical(row, *at)) + (inward + outward)

        return span, beyond

    def outer_rows(beyond, span, left):
        for j in range(1, left + 1):
            span(15 + j, 0, STEP)
            beyond(15 + j, left - j)

    for n in range(1, SWEEPS + 1):
        span, _ = sweeper(level[n - 1], level[n])
        for row in range(n, STEP - n):
            span(row, n, STEP - n)

    def put_prior(row, t, value):
        level0[row, t] = value

    fill_sides(DEPTH, put_prior, pcol, halo_recv.at[1])
    for n in range(1, SWEEPS + 1):
        span, beyond = sweeper(level[n - 1], level[n])
        for row in range(n, STEP - n):
            span(row, 0, n)
            span(row, STEP - n, STEP)
            beyond(row, DEPTH - n)
    fill_ends(DEPTH, lambda row, t: level0[row, t], put_prior, prow, pcorner, halo_recv)
    for n in range(1, SWEEPS + 1):
        span, beyond = sweeper(level[n - 1], level[n])
        for row in [*range(n), *range(STEP - n, STEP)]:
            span(row, 0, STEP)
            beyond(row, DEPTH - n)
        outer_rows(beyond, span, DEPTH - n)

    start_a(1, scatter([block_sums(level3, h) for h in range(2)]))
    start_b(0)

    def put_ids(row, t, value):
        ids[row, t] = value

    fill_sides(IDS, put_ids, zcol, zhalo_recv.at[1])
    fill_ends(IDS, lambda row, t: ids[row, t], put_ids, zrow, zcorner, zhalo_recv)

    def beside_ids(cells, own_cells):
        other = jnp.full((8, 128), -1, I32)
        for row, t in cells:
            value = ids[row, t]
            other = jnp.maximum(other, jnp.where(value == own_cells, -1, value))
        return jnp.where(lane[0:1] < 64, other[0:1], other[7:8])

    for h in range(2):
        cells = [(row, 15 + k) for row in range(8 * h, 8 * h + 8) for k in range(1, IDS + 1)]
        encode(beside_ids(cells, own[h]), 5 + h)
    lines, cells = own_ids(STEP)
    own.append(cells)
    encode(lines[0], 7)
    encode(lines[1], 8)
    corner = beside_ids([(15 + j, 15 + k) for j in range(1, IDS) for k in range(1, IDS + 1 - j)], own[2])
    encode(corner, 9)

    start_b(1)
    rate_copy.wait()
    target = rate_in[core] * finish_b(0)

    def lookup(table, groups):
        rows = jnp.dot(split2(table), onehot_lo[:, 0 : 128 * groups], preferred_element_type=F32)
        rows = rows[0:32] + rows[32:64]
        lines = []
        for g in range(groups):
            lines.append(spread(jnp.sum(rows[:, 128 * g : 128 * g + 128] * onehot_hi[g], axis=0, keepdims=True)))
        return lines

    def cell_factors(near, far, ext):
        mine = jnp.where(q < 4, near, far)
        next_block = jnp.where(lane >= 120, ext, pltpu.roll(near, 120, 1))
        return mine, jnp.where(q < 4, far, next_block)

    def factors_of(lines):
        ext = lines[4]
        return [cell_factors(lines[0], lines[1], ext), cell_factors(lines[2], lines[3], pltpu.roll(ext, 120, 1))]

    lines = lookup(share(0, target / finish_b(1)), GROUPS)
    pairs = factors_of(lines) + [cell_factors(lines[7], lines[8], lines[9])]
    sides = [lines[5], lines[6], lines[9]]
    for row in range(STEP + IDS):
        h = row // 8
        mine, east = pairs[h]
        scale = jnp.where(ids[row, 0:STEP] == own[h], mine, east)
        level3[row, 0:STEP] = level3[row, 0:STEP] * scale
        left = IDS if row < STEP else IDS - (row - 15)
        if left:
            reach = slice(STEP, STEP + left)
            scale = jnp.where(ids[row, reach] == own[h], mine, sides[h])
            level3[row, reach] = level3[row, reach] * scale

    for n in range(1, SWEEPS + 1):
        span, beyond = sweeper(level[(n + 2) % 4], level[n - 1] if n < SWEEPS else final)
        for row in range(STEP):
            span(row, 0, STEP)
            beyond(row, SWEEPS - n)
        outer_rows(beyond, span, SWEEPS - n)

    start_a(2, scatter([block_sums(final, h) for h in range(2)]))
    for r in range(STEP):
        slot = r % 4
        values = final[r]
        values = jnp.where(ids[r, 0:STEP] == own[r // 8], values, -values)
        for t in range(STEP):
            turn.at[slot][pl.ds(t, 8, stride=STEP), :] = values[t]
        rows = turn[slot].T
        for t in range(TILES):
            signed.at[t][pl.ds(r, 8, stride=STEP), :] = rows[8 * t : 8 * t + 8]
    start_b(2)
    pairs = factors_of(lookup(share(1, target / finish_b(2)), 5))
    for h in range(2):
        scales[2 * h] = pairs[h][0]
        scales[2 * h + 1] = -pairs[h][1]

    for sems, shapes in ((halo_send, (prow, pcol, pcorner)), (zhalo_send, (zrow, zcol, zcorner))):
        for m, ref in enumerate(shapes):
            drain(ref, sems.at[m])
    for n in range(3):
        drain(part_in.at[n, pl.ds(1, 7)], a_send.at[n])
        drain(half_in.at[n], b_send.at[n])
    for n in range(2):
        drain(factors.at[n, core], c_send.at[n])


def finish(signed, scales, out, lines, result, store_sem):
    for n in range(4):
        value = scales[n]
        cells = [jnp.broadcast_to(value[q : q + 1], (STEP, 128)) for q in range(8)]
        lines[n] = jnp.concatenate(cells, axis=0).T
    for t in range(TILES):
        for b in range(ROWS // 8):
            row, h = 8 * t + b // 2, b % 2
            value = signed[t, 8 * b : 8 * b + 8, :]
            mine = jnp.broadcast_to(lines[2 * h, row : row + 1, :], (8, 128))
            east = jnp.broadcast_to(lines[2 * h + 1, row : row + 1, :], (8, 128))
            result[t, 8 * b : 8 * b + 8, :] = value * jnp.where(value > 0, mine, east)
        pltpu.make_async_copy(result.at[t], out.at[:, 128 * t : 128 * t + 128], store_sem).start()
    drain(result, store_sem)


def body(prior, zone_ids, rate):
    dma = pltpu.SemaphoreType.DMA
    vmem = pltpu.VMEM
    outside = pl.BlockSpec(memory_space=pltpu.HBM)
    inside = pl.BlockSpec(memory_space=pltpu.VMEM)
    parts = pl.pallas_call(
        kernel,
        out_shape=(
            jax.ShapeDtypeStruct((TILES, ROWS, 128), F32),
            jax.ShapeDtypeStruct((4, 8, 128), F32),
        ),
        in_specs=[outside] * 3,
        out_specs=(inside, inside),
        scratch_shapes=[
            vmem((TILES, ROWS, 128), F32),
            vmem((TILES, ROWS, 128), I32),
            vmem((4, 128, 128), F32),
            vmem((4, 128, 128), I32),
            vmem((SIDE, SIDE, 8, 128), F32),
            vmem((SIDE, SIDE, 8, 128), F32),
            vmem((SIDE, SIDE, 8, 128), F32),
            vmem((SIDE, SIDE, 8, 128), F32),
            vmem((STEP, STEP, 8, 128), F32),
            vmem((STEP + IDS, STEP + IDS, 8, 128), I32),
            vmem((2, TILES, 8, 128), F32),
            vmem((2, 8, 128), F32),
            vmem((4, 8, 128), F32),
            vmem((2, TILES, 8, 128), I32),
            vmem((2, 8, 128), I32),
            vmem((4, 8, 128), I32),
            vmem((2, 8, 128), F32),
            vmem((2, 8, 128), I32),
            vmem((GROUPS, 32, 128), F32),
            vmem((128, 128 * GROUPS), BF16),
            vmem((3, 2, 16, 128), F32),
            vmem((3, 8, 16, 128), F32),
            vmem((3, 16, 128), F32),
            vmem((3, 15, 16, 128), F32),
            vmem((2, 2, 16, 128), F32),
            dma((2, 3)),
            dma,
            dma((3,)),
            dma((3,)),
            dma((3,)),
            dma((3,)),
            dma((3,)),
            dma((3,)),
            dma((3,)),
            dma((3,)),
            dma((2,)),
            dma((2,)),
            vmem((2, 16, 128), F32),
        ],
        compiler_params=pltpu.CompilerParams(
            collective_id=0, has_side_effects=True, vmem_limit_bytes=VMEM_LIMIT
        ),
    )(prior, zone_ids, rate.reshape(2, 16, 128))
    return pl.pallas_call(
        finish,
        out_shape=jax.ShapeDtypeStruct((ROWS, COLS), F32),
        in_specs=[inside, inside],
        out_specs=outside,
        scratch_shapes=[vmem((4, 128, 128), F32), vmem((TILES, ROWS, 128), F32), dma],
        compiler_params=pltpu.CompilerParams(vmem_limit_bytes=32 * 1024 * 1024),
    )(*parts)


def solution(mesh):
    placed = (P("lat", "lon"), P("lat", "lon"), P())
    return jax.shard_map(
        body, mesh=mesh, in_specs=placed, out_specs=P("lat", "lon"), check_vma=False
    )
```

```python
import jax
import jax.numpy as jnp
from jax import lax
from jax.experimental import pallas as pl
from jax.experimental.pallas import tpu as pltpu
from jax.sharding import PartitionSpec as P

ROWS, COLS = 128, 2048
STEP = 16
TILES = COLS // 128
SWEEPS = 3
DEPTH = 6
IDS = 3
SIDE = STEP + DEPTH
GROUPS = 10
VMEM_LIMIT = 55200000
MESH = pl.DeviceIdType.MESH
F32, I32, BF16 = jnp.float32, jnp.int32, jnp.bfloat16


def split2(x):
    high = x.astype(BF16)
    low = (x - high.astype(F32)).astype(BF16)
    return jnp.concatenate([high, low], axis=0)


def place(row, col):
    return {"lat": jnp.bitwise_and(row, 7), "lon": jnp.bitwise_and(col, 15)}


def device(x, core, y, z):
    return (jnp.bitwise_and(x, 3) * 2 + core, jnp.bitwise_and(y, 3) * 4 + jnp.bitwise_and(z, 3))


FAR_A = [2, 3, 1, 0]
FAR_B = sorted(
    [(a, b) for a in range(4) for b in range(4) if (a, b) != (0, 0)],
    key=lambda t: -(min(t[0], 4 - t[0]) + min(t[1], 4 - t[1])),
)


def drain(ref, sem):
    pltpu.make_async_copy(ref, ref, sem).wait()


def kernel(
    prior, zones, rate, signed, scales,
    pin, zin, turn, iturn, level0, level1, level2, level3, final, ids,
    prow, pcol, pcorner, zrow, zcol, zcorner, ppack, zpack,
    onehot_hi, onehot_lo,
    part, part_in, half, half_in, factors,
    load_sem, rate_sem, halo_send, halo_recv, zhalo_send, zhalo_recv,
    a_send, a_recv, b_send, b_recv, c_send, c_recv, rate_in,
):
    level = [level0, level1, level2, level3]
    lat, lon = lax.axis_index("lat"), lax.axis_index("lon")
    x, core = jnp.right_shift(lat, 1), jnp.bitwise_and(lat, 1)
    y, z = jnp.right_shift(lon, 2), jnp.bitwise_and(lon, 3)

    around = [(-1, 0), (1, 0), (0, -1), (0, 1), (-1, -1), (-1, 1), (1, -1), (1, 1)]
    a_peers = []
    for d in FAR_A:
        for flip in (1, 0):
            if (d, flip) != (0, 0):
                a_peers.append((d * 2 + flip, flip, device(x + d, 1 - core if flip else core, y, z)))
    b_peers = [(i, device(x, core, y + a, z + b)) for i, (a, b) in enumerate(FAR_B)]
    partner = device(x, 1 - core, y, z)

    barrier = pltpu.get_barrier_semaphore()
    greeted = 0
    for peer in [peer for _, peer in b_peers] + [peer for _, _, peer in a_peers] + [place(lat + dr, lon + dc) for dr, dc in around]:
        pl.semaphore_signal(barrier, inc=1, device_id=peer, device_id_type=MESH)
        greeted += 1

    def tile(t):
        return slice(128 * t, 128 * t + 128)

    for n, t in [(0, 0), (0, TILES - 1), (1, 0), (1, TILES - 1)] + [(n, t) for n in (0, 1) for t in range(1, TILES - 1)]:
        sem = load_sem.at[n, 0 if t == 0 else 1 if t == TILES - 1 else 2]
        pltpu.make_async_copy((prior, zones)[n].at[:, tile(t)], (pin, zin)[n].at[t], sem).start()
    rate_copy = pltpu.make_async_copy(rate, rate_in, rate_sem)
    rate_copy.start()

    lane = lax.broadcasted_iota(I32, (8, 128), 1)
    q = lax.broadcasted_iota(I32, (8, 128), 0)
    s = lax.rem(lane, 8)
    mirror_top = s + 8 * lat < 4
    mirror_bottom = s + 8 * lat >= 60

    def pick(value, index):
        return jnp.take_along_axis(value, index, axis=1, mode="promise_in_bounds")

    def spread(row, shape=(8, 128)):
        return jnp.broadcast_to(row, shape)

    inner = pl.ds(1, TILES - 2)

    def pack(ref, packed):
        index = 16 * s + lax.div(lane, 8)
        packed[0] = pick(ref[0].T[0:8], index)
        packed[1] = pick(ref[TILES - 1].T[120:128], index)

    first8, last8 = pl.ds(0, 8), pl.ds(ROWS - 8, 8)

    def send(src, dst, send_sem, recv_sem, dr, dc):
        pltpu.make_async_remote_copy(
            src_ref=src, dst_ref=dst, send_sem=send_sem, recv_sem=recv_sem,
            device_id=place(lat + dr, lon + dc), device_id_type=MESH,
        ).start()

    def send_rows(source, row_in, corner_in, out_sem, in_sem, depth):
        send(source.at[:, pl.ds(0, depth), :], row_in.at[1, :, pl.ds(0, depth), :], out_sem.at[0], in_sem.at[0], -1, 0)
        send(source.at[:, pl.ds(ROWS - depth, depth), :], row_in.at[0, :, pl.ds(8 - depth, depth), :], out_sem.at[0], in_sem.at[0], 1, 0)
        send(source.at[0, first8, :], corner_in.at[2], out_sem.at[2], in_sem.at[2], -1, -1)
        send(source.at[TILES - 1, first8, :], corner_in.at[3], out_sem.at[2], in_sem.at[2], -1, 1)
        send(source.at[0, last8, :], corner_in.at[0], out_sem.at[2], in_sem.at[2], 1, -1)
        send(source.at[TILES - 1, last8, :], corner_in.at[1], out_sem.at[2], in_sem.at[2], 1, 1)

    def send_cols(packed, col_in, out_sem, in_sem):
        send(packed.at[0], col_in.at[0], out_sem.at[1], in_sem.at[1], 0, -1)
        send(packed.at[1], col_in.at[1], out_sem.at[1], in_sem.at[1], 0, 1)

    drain(pin.at[0], load_sem.at[0, 0])
    drain(pin.at[TILES - 1], load_sem.at[0, 1])
    pack(pin, ppack)
    drain(pin.at[inner], load_sem.at[0, 2])
    pl.semaphore_wait(barrier, greeted)
    send_cols(ppack, pcol, halo_send, halo_recv)
    send_rows(pin, prow, pcorner, halo_send, halo_recv, DEPTH)

    def turned(matrix, slot):
        buffer = turn if matrix.dtype == F32 else iturn
        buffer[slot] = matrix.T
        return [buffer.at[slot][pl.ds(t, 8, stride=STEP), :] for t in range(STEP)]

    def load_planes(ref, write):
        for r in range(STEP):
            rows = [ref.at[t][pl.ds(r, 8, stride=STEP), :] for t in range(TILES)]
            for t, value in enumerate(turned(jnp.concatenate(rows, axis=0), r % 4)):
                write(r, t, value)

    def write_prior(r, t, value):
        level0[r, t] = value

    def write_ids(r, t, value):
        ids[r, t] = value

    load_planes(pin, write_prior)
    drain(zin.at[0], load_sem.at[1, 0])
    drain(zin.at[TILES - 1], load_sem.at[1, 1])
    pack(zin, zpack)
    drain(zin.at[inner], load_sem.at[1, 2])
    send_cols(zpack, zcol, zhalo_send, zhalo_recv)
    send_rows(zin, zrow, zcorner, zhalo_send, zhalo_recv, IDS)
    load_planes(zin, write_ids)

    hi_iota = lax.broadcasted_iota(I32, (32, 128), 0)
    lo_iota = lax.broadcasted_iota(I32, (128, 128), 0)

    def encode(line, group):
        hi = jnp.right_shift(line, 7)
        lo = jnp.bitwise_and(line, 127)
        onehot_hi[group] = jnp.where(hi_iota == hi, 1.0, 0.0)
        onehot_lo[:, 128 * group : 128 * group + 128] = jnp.where(lo_iota == lo, 1.0, 0.0).astype(BF16)

    def own_ids(row):
        value = ids[row, 0]
        return [value[0:1], value[4:5]], jnp.where(q < 4, spread(value[0:1]), spread(value[4:5]))

    own = []
    for h in range(2):
        lines, cells = own_ids(8 * h)
        own.append(cells)
        for g in range(2):
            encode(lines[g], 2 * h + g)

    def fold(value):
        value = value + pltpu.roll(value, 7, 0)
        value = value + pltpu.roll(value, 6, 0)
        return value[0:1], value[4:5]

    def scatter(pairs):
        lines, ext = [], []
        for own_sum, east_sum in pairs:
            own0, own1 = fold(own_sum)
            east0, east1 = fold(east_sum)
            east1 = spread(east1)
            beyond = pltpu.roll(east1, 8, 1)[0:1]
            lines.append(own0 + jnp.where(lane[0:1] >= 8, beyond, 0.0))
            lines.append(own1 + east0)
            ext.append((east1[0:1], beyond))
        lines.append(jnp.where(lane[0:1] >= 120, ext[0][0], jnp.where(lane[0:1] < 8, ext[1][1], 0.0)))
        weighted = split2(jnp.concatenate([onehot_hi[g] * lines[g] for g in range(5)], axis=1))
        table = lax.dot_general(
            weighted, onehot_lo[:, 0:640], (((1,), (1,)), ((), ())), preferred_element_type=F32
        )
        return table[0:32] + table[32:64]

    def block_sums(source, h):
        own_sum, east_sum = jnp.zeros((STEP, 8, 128), F32), jnp.zeros((STEP, 8, 128), F32)
        for r in range(8 * h, 8 * h + 8):
            matched = ids[r, 0:STEP] == own[h]
            value = source[r, 0:STEP]
            own_sum += jnp.where(matched, value, 0.0)
            east_sum += jnp.where(matched, 0.0, value)
        return jnp.sum(own_sum, axis=0), jnp.sum(east_sum, axis=0)

    counts, others = [], []
    for h in range(2):
        own_sum = jnp.zeros((STEP, 8, 128), F32)
        other = jnp.full((STEP, 8, 128), -1, I32)
        for r in range(8 * h, 8 * h + 8):
            value = ids[r, 0:STEP]
            matched = value == own[h]
            own_sum += jnp.where(matched, 1.0, 0.0)
            other = jnp.maximum(other, jnp.where(matched, -1, value))
        own_sum = jnp.sum(own_sum, axis=0)
        counts.append((own_sum, float(8 * STEP) - own_sum))
        others.append(spread(jnp.max(other, axis=0)[7:8]))
    encode(jnp.where(lane >= 120, others[0], jnp.where(lane < 8, pltpu.roll(others[1], 8, 1), -1))[0:1], 4)

    def start_a(n, table):
        part[n] = table.reshape(2, 16, 128)
        for slot, flip, peer in a_peers:
            pltpu.make_async_remote_copy(
                src_ref=part.at[n, 1 - core if flip else core], dst_ref=part_in.at[n, slot],
                send_sem=a_send.at[n], recv_sem=a_recv.at[n], device_id=peer, device_id_type=MESH,
            ).start()

    def start_b(n):
        drain(part_in.at[n, pl.ds(1, 7)], a_recv.at[n])
        total = part[n, core]
        for slot in range(1, 8):
            total += part_in[n, slot]
        half[n] = total
        for i, peer in b_peers:
            pltpu.make_async_remote_copy(
                src_ref=half.at[n], dst_ref=half_in.at[n, i],
                send_sem=b_send.at[n], recv_sem=b_recv.at[n], device_id=peer, device_id_type=MESH,
            ).start()

    def finish_b(n):
        drain(half_in.at[n], b_recv.at[n])
        total = half[n]
        for i in range(15):
            total += half_in[n, i]
        return total

    def share(n, factor):
        factors[n, core] = factor
        pltpu.make_async_remote_copy(
            src_ref=factors.at[n, core], dst_ref=factors.at[n, core],
            send_sem=c_send.at[n], recv_sem=c_recv.at[n], device_id=partner, device_id_type=MESH,
        ).start()
        drain(factors.at[n, 1 - core], c_recv.at[n])
        return factors[n].reshape(32, 128)

    start_a(0, scatter(counts))

    def fill_sides(depth, put, col_in, sem):
        drain(col_in, sem)
        east = pltpu.roll(col_in[0], 120, 1)
        west = col_in[1]
        for k in range(1, depth + 1):
            both = jnp.where(q < 4, spread(west[8 - k : 9 - k]), spread(east[k - 1 : k]))
            for r in range(STEP):
                put(r, 15 + k, pltpu.roll(both, (128 - 8 * r) % 128, 1) if r else both)

    def fill_ends(depth, get, put, row_in, corner_in, sems):
        def mirrored(j, t, value):
            return jnp.where(mirror_top, get(j - 1, t), jnp.where(mirror_bottom, get(STEP - j, t), value))

        drain(corner_in, sems.at[2])
        for k in range(1, depth):
            near, far = jnp.full((8, 128), k - 1, I32), jnp.full((8, 128), 128 - k, I32)
            north = jnp.where(lane < 64, pick(corner_in[1], far), pick(corner_in[0], near))
            south = jnp.where(lane < 64, pick(corner_in[3], far), pick(corner_in[2], near))
            for j in range(1, depth + 1 - k):
                value = jnp.where(s < 4, spread(north[8 - j : 9 - j]), spread(south[j - 1 : j]))
                put(15 + j, 15 + k, mirrored(j, 15 + k, value))
        drain(row_in.at[:, :, pl.ds(0, depth), :], sems.at[0])
        for j in range(1, depth + 1):
            rows = []
            for t in range(TILES):
                north, south = row_in[0, t, 8 - j : 9 - j, :], row_in[1, t, j - 1 : j, :]
                rows.append(jnp.where(q < 4, spread(north), spread(south)))
            for t, value in enumerate(turned(jnp.concatenate(rows, axis=0), j % 4)):
                put(15 + j, t, mirrored(j, t, value))

    def sweeper(src, dst):
        def get(row, a, b):
            return src[row, a:b]

        def vertical(row, a, b):
            if row == 0:
                north = jnp.where(s == 0, get(STEP, a, b), pltpu.roll(get(STEP - 1, a, b), 1, 2))
                return north + get(1, a, b)
            if row == STEP - 1:
                south = jnp.where(s == 7, get(STEP, a, b), pltpu.roll(get(0, a, b), 127, 2))
                return get(STEP - 2, a, b) + south
            if row == STEP:
                return jnp.where(s < 4, get(0, a, b), get(STEP - 1, a, b)) + get(STEP + 1, a, b)
            return get(row - 1, a, b) + get(row + 1, a, b)

        def west_edge(row):
            value = pltpu.roll(src[row, STEP - 1], 1, 0)
            return jnp.where(q == 0, jnp.where(lane < 8, src[row, STEP], pltpu.roll(value, 8, 1)), value)[None]

        def east_edge(row):
            value = pltpu.roll(src[row, 0], 7, 0)
            return jnp.where(q == 7, jnp.where(lane >= 120, src[row, STEP], pltpu.roll(value, 120, 1)), value)[None]

        def span(row, a, b):
            lo, hi = max(a - 1, 0), min(b + 1, STEP)
            values = get(row, lo, hi)
            centre = values[a - lo : b - lo]
            west = [values[0 : b - 1 - lo]] if b - 1 > lo else []
            east = [values[a + 1 - lo :]] if a + 1 < hi else []
            west = jnp.concatenate(west if a > 0 else [west_edge(row)] + west, axis=0)
            east = jnp.concatenate(east if b < STEP else east + [east_edge(row)], axis=0)
            dst[row, a:b] = (centre + vertical(row, a, b)) + (west + east)

        def beyond(row, count):
            for k in range(1, count + 1):
                if k == 1:
                    inward = jnp.where(q < 4, src[row, 0], src[row, STEP - 1])[None]
                else:
                    inward = get(row, 14 + k, 15 + k)
                outward = get(row, 16 + k, 17 + k)
                at = (15 + k, 16 + k)
                dst[row, at[0] : at[1]] = (get(row, *at) + vertical(row, *at)) + (inward + outward)

        return span, beyond

    def outer_rows(beyond, span, left):
        for j in range(1, left + 1):
            span(15 + j, 0, STEP)
            beyond(15 + j, left - j)

    for n in range(1, SWEEPS + 1):
        span, _ = sweeper(level[n - 1], level[n])
        for row in range(n, STEP - n):
            span(row, n, STEP - n)

    def put_prior(row, t, value):
        level0[row, t] = value

    fill_sides(DEPTH, put_prior, pcol, halo_recv.at[1])
    for n in range(1, SWEEPS + 1):
        span, beyond = sweeper(level[n - 1], level[n])
        for row in range(n, STEP - n):
            span(row, 0, n)
            span(row, STEP - n, STEP)
            beyond(row, DEPTH - n)
    fill_ends(DEPTH, lambda row, t: level0[row, t], put_prior, prow, pcorner, halo_recv)
    for n in range(1, SWEEPS + 1):
        span, beyond = sweeper(level[n - 1], level[n])
        for row in [*range(n), *range(STEP - n, STEP)]:
            span(row, 0, STEP)
            beyond(row, DEPTH - n)
        outer_rows(beyond, span, DEPTH - n)

    start_a(1, scatter([block_sums(level3, h) for h in range(2)]))
    start_b(0)

    def put_ids(row, t, value):
        ids[row, t] = value

    fill_sides(IDS, put_ids, zcol, zhalo_recv.at[1])
    fill_ends(IDS, lambda row, t: ids[row, t], put_ids, zrow, zcorner, zhalo_recv)

    def beside_ids(cells, own_cells):
        other = jnp.full((8, 128), -1, I32)
        for row, t in cells:
            value = ids[row, t]
            other = jnp.maximum(other, jnp.where(value == own_cells, -1, value))
        return jnp.where(lane[0:1] < 64, other[0:1], other[7:8])

    for h in range(2):
        cells = [(row, 15 + k) for row in range(8 * h, 8 * h + 8) for k in range(1, IDS + 1)]
        encode(beside_ids(cells, own[h]), 5 + h)
    lines, cells = own_ids(STEP)
    own.append(cells)
    encode(lines[0], 7)
    encode(lines[1], 8)
    corner = beside_ids([(15 + j, 15 + k) for j in range(1, IDS) for k in range(1, IDS + 1 - j)], own[2])
    encode(corner, 9)

    start_b(1)
    rate_copy.wait()
    target = rate_in[core] * finish_b(0)

    def lookup(table, groups):
        rows = jnp.dot(split2(table), onehot_lo[:, 0 : 128 * groups], preferred_element_type=F32)
        rows = rows[0:32] + rows[32:64]
        lines = []
        for g in range(groups):
            lines.append(spread(jnp.sum(rows[:, 128 * g : 128 * g + 128] * onehot_hi[g], axis=0, keepdims=True)))
        return lines

    def cell_factors(near, far, ext):
        mine = jnp.where(q < 4, near, far)
        next_block = jnp.where(lane >= 120, ext, pltpu.roll(near, 120, 1))
        return mine, jnp.where(q < 4, far, next_block)

    def factors_of(lines):
        ext = lines[4]
        return [cell_factors(lines[0], lines[1], ext), cell_factors(lines[2], lines[3], pltpu.roll(ext, 120, 1))]

    lines = lookup(share(0, target / finish_b(1)), GROUPS)
    pairs = factors_of(lines) + [cell_factors(lines[7], lines[8], lines[9])]
    sides = [lines[5], lines[6], lines[9]]
    for row in range(STEP + IDS):
        h = row // 8
        mine, east = pairs[h]
        scale = jnp.where(ids[row, 0:STEP] == own[h], mine, east)
        level3[row, 0:STEP] = level3[row, 0:STEP] * scale
        left = IDS if row < STEP else IDS - (row - 15)
        if left:
            reach = slice(STEP, STEP + left)
            scale = jnp.where(ids[row, reach] == own[h], mine, sides[h])
            level3[row, reach] = level3[row, reach] * scale

    for n in range(1, SWEEPS + 1):
        span, beyond = sweeper(level[(n + 2) % 4], level[n - 1] if n < SWEEPS else final)
        for row in range(STEP):
            span(row, 0, STEP)
            beyond(row, SWEEPS - n)
        outer_rows(beyond, span, SWEEPS - n)

    start_a(2, scatter([block_sums(final, h) for h in range(2)]))
    for r in range(STEP):
        slot = r % 4
        values = final[r]
        values = jnp.where(ids[r, 0:STEP] == own[r // 8], values, -values)
        for t in range(STEP):
            turn.at[slot][pl.ds(t, 8, stride=STEP), :] = values[t]
        rows = turn[slot].T
        for t in range(TILES):
            signed.at[t][pl.ds(r, 8, stride=STEP), :] = rows[8 * t : 8 * t + 8]
    start_b(2)
    pairs = factors_of(lookup(share(1, target / finish_b(2)), 5))
    for h in range(2):
        scales[2 * h] = pairs[h][0]
        scales[2 * h + 1] = -pairs[h][1]

    shapes0 = (prow.at[:, :, pl.ds(0, DEPTH), :], pcol, pcorner)
    shapes1 = (zrow.at[:, :, pl.ds(0, IDS), :], zcol, zcorner)
    for sems, shapes in ((halo_send, shapes0), (zhalo_send, shapes1)):
        for m, ref in enumerate(shapes):
            drain(ref, sems.at[m])
    for n in range(3):
        drain(part_in.at[n, pl.ds(1, 7)], a_send.at[n])
        drain(half_in.at[n], b_send.at[n])
    for n in range(2):
        drain(factors.at[n, core], c_send.at[n])


def finish(signed, scales, out, lines, result, store_sem):
    for n in range(4):
        value = scales[n]
        cells = [jnp.broadcast_to(value[q : q + 1], (STEP, 128)) for q in range(8)]
        lines[n] = jnp.concatenate(cells, axis=0).T
    for t in range(TILES):
        for b in range(ROWS // 8):
            row, h = 8 * t + b // 2, b % 2
            value = signed[t, 8 * b : 8 * b + 8, :]
            mine = jnp.broadcast_to(lines[2 * h, row : row + 1, :], (8, 128))
            east = jnp.broadcast_to(lines[2 * h + 1, row : row + 1, :], (8, 128))
            result[t, 8 * b : 8 * b + 8, :] = value * jnp.where(value > 0, mine, east)
        pltpu.make_async_copy(result.at[t], out.at[:, 128 * t : 128 * t + 128], store_sem).start()
    drain(result, store_sem)


def body(prior, zone_ids, rate):
    dma = pltpu.SemaphoreType.DMA
    vmem = pltpu.VMEM
    outside = pl.BlockSpec(memory_space=pltpu.HBM)
    inside = pl.BlockSpec(memory_space=pltpu.VMEM)
    parts = pl.pallas_call(
        kernel,
        out_shape=(
            jax.ShapeDtypeStruct((TILES, ROWS, 128), F32),
            jax.ShapeDtypeStruct((4, 8, 128), F32),
        ),
        in_specs=[outside] * 3,
        out_specs=(inside, inside),
        scratch_shapes=[
            vmem((TILES, ROWS, 128), F32),
            vmem((TILES, ROWS, 128), I32),
            vmem((4, 128, 128), F32),
            vmem((4, 128, 128), I32),
            vmem((SIDE, SIDE, 8, 128), F32),
            vmem((SIDE, SIDE, 8, 128), F32),
            vmem((SIDE, SIDE, 8, 128), F32),
            vmem((SIDE, SIDE, 8, 128), F32),
            vmem((STEP, STEP, 8, 128), F32),
            vmem((STEP + IDS, STEP + IDS, 8, 128), I32),
            vmem((2, TILES, 8, 128), F32),
            vmem((2, 8, 128), F32),
            vmem((4, 8, 128), F32),
            vmem((2, TILES, 8, 128), I32),
            vmem((2, 8, 128), I32),
            vmem((4, 8, 128), I32),
            vmem((2, 8, 128), F32),
            vmem((2, 8, 128), I32),
            vmem((GROUPS, 32, 128), F32),
            vmem((128, 128 * GROUPS), BF16),
            vmem((3, 2, 16, 128), F32),
            vmem((3, 8, 16, 128), F32),
            vmem((3, 16, 128), F32),
            vmem((3, 15, 16, 128), F32),
            vmem((2, 2, 16, 128), F32),
            dma((2, 3)),
            dma,
            dma((3,)),
            dma((3,)),
            dma((3,)),
            dma((3,)),
            dma((3,)),
            dma((3,)),
            dma((3,)),
            dma((3,)),
            dma((2,)),
            dma((2,)),
            vmem((2, 16, 128), F32),
        ],
        compiler_params=pltpu.CompilerParams(
            collective_id=0, has_side_effects=True, vmem_limit_bytes=VMEM_LIMIT
        ),
    )(prior, zone_ids, rate.reshape(2, 16, 128))
    return pl.pallas_call(
        finish,
        out_shape=jax.ShapeDtypeStruct((ROWS, COLS), F32),
        in_specs=[inside, inside],
        out_specs=outside,
        scratch_shapes=[vmem((4, 128, 128), F32), vmem((TILES, ROWS, 128), F32), dma],
        compiler_params=pltpu.CompilerParams(vmem_limit_bytes=32 * 1024 * 1024),
    )(*parts)


def solution(mesh):
    placed = (P("lat", "lon"), P("lat", "lon"), P())
    return jax.shard_map(
        body, mesh=mesh, in_specs=placed, out_specs=P("lat", "lon"), check_vma=False
    )
```
